32 devices in a mesh: segment: 8 (over z, y), band: 4 (over x, core).
Axes of the slice: x: 2, y: 2, z: 4, core: 2. Of those that a mesh axis runs over, the one named last changes fastest.
Arguments:
- forward_state: bfloat16 [8, 2, 32, 64, 256], P('segment', None, 'band'), may hold values from -6 to 6
- returning_state: bfloat16 [8, 2, 32, 64, 256], P('segment', None, 'band'), may hold values from -6 to 6
- returning_grad: bfloat16 [8, 2, 32, 64, 256], P('segment', None, 'band'), may hold values from -6 to 6
- weights: bfloat16 [8, 2, 2304, 256], P('segment'), may hold values from -0.125 to 0.125
- fresh_input: bfloat16 [2, 2, 32, 64, 256], P(None, None, 'band'), may hold values from -6 to 6
- loss_grad: bfloat16 [2, 2, 32, 64, 256], P(None, None, 'band'), may hold values from -6 to 6
Outputs:
- forward_out: bfloat16 [8, 2, 32, 64, 256], P('segment', None, 'band')
- returning_out: bfloat16 [8, 2, 32, 64, 256], P('segment', None, 'band')
- backward_out: bfloat16 [8, 2, 32, 64, 256], P('segment', None, 'band')
- weight_grad: float32 [8, 2, 2304, 256], P('segment', None, 'band')
The draws below stay inside these ranges and needn't reach their ends.
All inputs are finite; a program needn't handle non-finite values.
Results may differ from the reference program's by a relative error of at most 0.02.
Values may be sent and summed in bfloat16 or wider, within the bound.
A program may use at most 64 MiB of HBM per device.

```python
import jax
import jax.numpy as jnp
from jax import lax

CHANNELS = 256
TILE_COLS = 64
TICK_COUNT = 2
SEGMENTS = 8
HEIGHT = 32


def shard_levels(rng, shape, split, low, largest):
    def one(axis_at, shards_of):
        heights = jax.random.uniform(jax.random.fold_in(jax.random.fold_in(rng, 6), axis_at), (shards_of,), jnp.float32, low / len(split), largest / len(split))
        return jnp.repeat(jnp.exp(heights), shape[axis_at] // shards_of).reshape((-1,) + (1,) * (len(shape) - axis_at - 1))

    loudness = one(*split[0])
    for cut in split[1:]:
        loudness = loudness * one(*cut)
    return loudness


def noise(own_key, dims, deviation, most, shards=(), dtype=jnp.bfloat16):
    values = jax.random.normal(own_key, dims, jnp.float32) * deviation
    if len(shards) > 0:
        values = shard_levels(own_key, dims, shards, -0.22, 0.18) * values
    return jnp.clip(values, min=-most, max=most).astype(dtype)


def setup_inputs(seed: int = 0) -> dict:
    splits = jax.random.split(jax.random.key(seed), 7)
    return {
        "forward_state": noise(splits[0], (SEGMENTS, 2, HEIGHT, TILE_COLS, CHANNELS), 1.0, 6.0, ((0, 8), (2, 4))),
        "returning_state": noise(splits[1], (SEGMENTS, 2, HEIGHT, TILE_COLS, CHANNELS), 1.0, 6.0, ((0, 8), (2, 4))),
        "returning_grad": noise(splits[2], (SEGMENTS, 2, HEIGHT, TILE_COLS, CHANNELS), 1.0, 6.0, ((0, 8), (2, 4))),
        "weights": noise(splits[3], (SEGMENTS, 2, 9 * CHANNELS, CHANNELS), (9 * CHANNELS) ** -0.5, 0.125, ((0, 8),)),
        "fresh_input": noise(splits[4], (TICK_COUNT, 2, HEIGHT, TILE_COLS, CHANNELS), 1.0, 6.0, ((2, 4),)),
        "loss_grad": noise(splits[5], (TICK_COUNT, 2, HEIGHT, TILE_COLS, CHANNELS), 1.0, 6.0, ((2, 4),)),
    }


def activate(values):
    return jax.nn.silu(values.astype(jnp.float32)).astype(jnp.bfloat16)


def silu_slope(values):
    sigmoid = jax.nn.sigmoid(values)
    return sigmoid * (1.0 + values * (1.0 - sigmoid))


def rows_padded(field):
    return jnp.pad(field, ((1, 1), (0, 0), (0, 0)))


def gather_taps(rowpadded, flipped):
    height = rowpadded.shape[0] - 2
    across = rowpadded.shape[1]
    padded = jnp.pad(rowpadded, ((0, 0), (1, 1), (0, 0)))
    pieces = []
    for first in range(3):
        for second in range(3):
            if flipped:
                row_start, col_start = 2 - first, 2 - second
            else:
                row_start, col_start = first, second
            pieces.append(padded[row_start:row_start + height, col_start:col_start + across, :])
    return jnp.concatenate(pieces, -1).reshape(height * across, -1)


def apply_taps(taps_matrix, weight):
    return jnp.dot(taps_matrix, weight, preferred_element_type=jnp.float32)


def flip_weight(weight, channels):
    return weight.reshape(9, channels, channels).transpose(0, 2, 1).reshape(9 * channels, channels)


def correlate(taps_matrix, grads):
    return lax.dot_general(taps_matrix, grads, (((0,), (0,)), ((), ())), preferred_element_type=jnp.float32)


def forward_block(inputs, weight_f, weight_g):
    first_in, second_in = inputs[0], inputs[1]
    shape = first_in.shape
    taps_f = gather_taps(rows_padded(activate(second_in)), False)
    first_out = (first_in.astype(jnp.float32) + apply_taps(taps_f, weight_f).reshape(shape)).astype(jnp.bfloat16)
    taps_g = gather_taps(rows_padded(activate(first_out)), False)
    second_out = (second_in.astype(jnp.float32) + apply_taps(taps_g, weight_g).reshape(shape)).astype(jnp.bfloat16)
    return jnp.stack([first_out, second_out])


def backward_block(outputs, grads, weight_f, weight_g):
    first_out, second_out = outputs[0], outputs[1]
    first_grad, second_grad = grads[0], grads[1]
    shape = first_out.shape
    channels = shape[2]
    taps_g = gather_taps(rows_padded(activate(first_out)), False)
    second_in = (second_out.astype(jnp.float32) - apply_taps(taps_g, weight_g).reshape(shape)).astype(jnp.bfloat16)
    taps_f = gather_taps(rows_padded(activate(second_in)), False)
    first_in = (first_out.astype(jnp.float32) - apply_taps(taps_f, weight_f).reshape(shape)).astype(jnp.bfloat16)
    back_g = apply_taps(gather_taps(rows_padded(second_grad), True), flip_weight(weight_g, channels)).reshape(shape)
    first_back = (first_grad.astype(jnp.float32) + silu_slope(first_out.astype(jnp.float32)) * back_g).astype(jnp.bfloat16)
    back_f = apply_taps(gather_taps(rows_padded(first_back), True), flip_weight(weight_f, channels)).reshape(shape)
    second_back = (second_grad.astype(jnp.float32) + silu_slope(second_in.astype(jnp.float32)) * back_f).astype(jnp.bfloat16)
    grad_f = correlate(taps_f, first_back.reshape(-1, channels))
    grad_g = correlate(taps_g, second_grad.reshape(-1, channels))
    return jnp.stack([first_in, second_in]), jnp.stack([first_back, second_back]), jnp.stack([grad_f, grad_g])


def one_segment(pieces):
    state, outputs, grads, weight = pieces
    advanced = forward_block(state, weight[0], weight[1])
    inverted, backed, wgrad = backward_block(outputs, grads, weight[0], weight[1])
    return advanced, inverted, backed, wgrad


def reference(forward_state, returning_state, returning_grad, weights, fresh_input, loss_grad):
    totals = jnp.zeros((SEGMENTS, 2, 9 * CHANNELS, CHANNELS), jnp.float32)
    for tick_index in range(TICK_COUNT):
        advanced, inverted, backed, wgrad = lax.map(one_segment, (forward_state, returning_state, returning_grad, weights))
        totals = totals + wgrad
        forward_state = jnp.concatenate([fresh_input[tick_index][None], advanced[:-1]], 0)
        returning_state = jnp.concatenate([inverted[1:], advanced[-1:]], 0)
        returning_grad = jnp.concatenate([backed[1:], loss_grad[tick_index][None]], 0)
    return forward_state, returning_state, returning_grad, totals
```

```python
import functools

import jax
import jax.numpy as jnp
from jax import lax
from jax.experimental import pallas as pl
from jax.experimental.pallas import tpu as pltpu
from jax.sharding import PartitionSpec as P

MESH = pl.DeviceIdType.MESH
ACT_Q, ACT_OUT, ACT_Y, GRAD2, ACT_IN, BACK1 = range(6)
FWD1, FWD2, RET1, RET2, GRD1, GRD2 = range(6)
F, G = 0, 1
OWN, OTHER = 0, 1
DEPTH = {FWD1: 1, FWD2: 2, RET1: 2, RET2: 1, GRD1: 1, GRD2: 2}


def kernel(segments, bands, width, pieces, fwd_in, ret_in, grd_in, weights_in, fresh_in, loss_in,
           fwd_out, ret_out, grd_out, wgrad_out,
           fields, wts, stack, sent, total, total_half, paired, reduced, partial, owned, ship_src, ship_dst,
           in_sem, w_sem, edge_sem, halo_send, halo_recv, mid_send, mid_recv, end_send, end_recv,
           wy_send, wy_recv, wx_send, wx_recv, wc_send, wc_recv,
           pair_send, pair_recv, red_send, red_recv, ship_send, ship_recv):
    seg = lax.axis_index("segment")
    band = lax.axis_index("band")
    pixels = sent.shape[2]
    channels = sent.shape[3]
    triple = 3 * channels
    chunk = partial.shape[3]
    margin = 2 * width
    inner = pl.ds(margin, pixels)
    first_pixels = pixels + 2 * width
    parity = lax.rem(seg, 2)
    even, odd = parity == 0, parity == 1
    other_seg = seg + 1 - 2 * parity
    first_seg, last_seg = seg == 0, seg == segments - 1
    below, above = seg >= 2, seg < segments - 2
    groups = bands // 2
    core, group = lax.rem(band, 2), band // 2
    core_band = band + 1 - 2 * core
    at_top, at_bottom = band == 0, band == bands - 1

    sources = {FWD1: fwd_in.at[0], FWD2: fwd_in.at[1], RET1: ret_in.at[0], RET2: ret_in.at[1],
               GRD1: grd_in.at[0], GRD2: grd_in.at[1]}

    def load(field):
        return pltpu.make_async_copy(sources[field], fields.at[0, field, inner], in_sem.at[field])

    def load_weights(index):
        return pltpu.make_async_copy(weights_in.at[index], wts.at[OWN, index], w_sem.at[index])

    load(RET1).start()
    load(GRD2).start()
    load_weights(G).start()
    load(RET2).start()
    load(GRD1).start()
    load_weights(F).start()
    load(FWD2).start()
    load(FWD1).start()

    barrier = pltpu.get_barrier_semaphore()
    for step in range(1, bands):
        pl.semaphore_signal(barrier, inc=1, device_id=(seg, lax.rem(band + step, bands)), device_id_type=MESH)
    pl.semaphore_signal(barrier, inc=1, device_id=(other_seg, band), device_id_type=MESH)

    @pl.when(below)
    def _():
        pl.semaphore_signal(barrier, inc=1, device_id=(seg - 2, band), device_id_type=MESH)

    @pl.when(above)
    def _():
        pl.semaphore_signal(barrier, inc=1, device_id=(seg + 2, band), device_id_type=MESH)

    def edge(which):
        return (
            pltpu.make_async_copy(fresh_in.at[0], fields.at[1, pl.ds(FWD1, 2), inner], edge_sem.at[0]),
            pltpu.make_async_copy(fresh_in.at[1], fwd_out, edge_sem.at[1]),
            pltpu.make_async_copy(loss_in.at[0], fields.at[1, pl.ds(GRD1, 2), inner], edge_sem.at[2]),
            pltpu.make_async_copy(loss_in.at[1], grd_out, edge_sem.at[3]),
        )[which]

    edge_places = (seg == 1, first_seg, seg == segments - 2, last_seg)
    for which in range(4):
        pl.when(edge_places[which])(edge(which).start)

    @pl.when(at_top)
    def _():
        fields[:, :, 0:margin] = jnp.zeros((2, 6, margin, channels), jnp.bfloat16)

    @pl.when(at_bottom)
    def _():
        fields[:, :, margin + pixels:] = jnp.zeros((2, 6, margin, channels), jnp.bfloat16)

    def halo_copy(tick, field, side):
        size = DEPTH[field] * width
        if side == 0:
            source, target = margin, margin + pixels
        else:
            source, target = margin + pixels - size, margin - size
        return pltpu.make_async_remote_copy(
            src_ref=fields.at[tick, field, pl.ds(source, size)], dst_ref=fields.at[tick, field, pl.ds(target, size)],
            send_sem=halo_send.at[tick, field, side], recv_sem=halo_recv.at[tick, field, 1 - side],
            device_id=(seg, band - 1 if side == 0 else band + 1), device_id_type=MESH)

    def send_halo(tick, field):
        pl.when(jnp.logical_not(at_top))(halo_copy(tick, field, 0).start)
        pl.when(jnp.logical_not(at_bottom))(halo_copy(tick, field, 1).start)

    def take_halo(tick, field):
        pl.when(jnp.logical_not(at_top))(halo_copy(tick, field, 1).wait_recv)
        pl.when(jnp.logical_not(at_bottom))(halo_copy(tick, field, 0).wait_recv)

    piece = chunk // pieces

    def w_rows(owner, part):
        return pl.ds(pl.multiple_of(owner * chunk + part * piece, piece), piece)

    def w_across(index, part):
        return pltpu.make_async_remote_copy(
            src_ref=wts.at[OWN, index, w_rows(band, part)], dst_ref=wts.at[OTHER, index, w_rows(band, part)],
            send_sem=wy_send.at[index, part], recv_sem=wy_recv.at[index, part],
            device_id=(other_seg, band), device_id_type=MESH)

    def w_group(index, part, step):
        rows = w_rows(band, part)
        return pltpu.make_async_remote_copy(
            src_ref=wts.at[OTHER, index, rows], dst_ref=wts.at[OTHER, index, rows],
            send_sem=wx_send.at[index, part, step - 1], recv_sem=wx_recv.at[index, part, step - 1],
            device_id=(seg, 2 * lax.rem(group + step, groups) + core), device_id_type=MESH)

    def w_core(index, part, step):
        rows = w_rows(2 * lax.rem(group + groups - step, groups) + core, part)
        return pltpu.make_async_remote_copy(
            src_ref=wts.at[OTHER, index, rows], dst_ref=wts.at[OTHER, index, rows],
            send_sem=wc_send.at[index, part, step], recv_sem=wc_recv.at[index, part, step],
            device_id=(seg, core_band), device_id_type=MESH)

    def spread_weights(index, part):
        w_across(index, part).wait_recv()
        for step in range(1, groups):
            w_group(index, part, step).start()
        w_core(index, part, 0).start()

    def pass_weights(index, part):
        for step in range(1, groups):
            w_group(index, part, step).wait_recv()
            w_core(index, part, step).start()

    def take_weights(index):
        for part in range(pieces):
            for step in range(groups):
                w_core(index, part, step).wait_recv()

    def fill(slot, value):
        rows = value.shape[0]
        column = lax.rem(lax.broadcasted_iota(jnp.int32, (rows, channels), 0), width)
        wide = value.astype(jnp.float32)
        left = jnp.where(column == 0, 0.0, pltpu.roll(wide, 1, 0))
        right = jnp.where(column == width - 1, 0.0, pltpu.roll(wide, rows - 1, 0))
        stack[slot, 0:rows, 0:channels] = left.astype(jnp.bfloat16)
        stack[slot, 0:rows, channels:2 * channels] = value
        stack[slot, 0:rows, 2 * channels:triple] = right.astype(jnp.bfloat16)

    def conv(slot, weight, rows):
        result = None
        for row in range(3):
            term = jnp.dot(stack[slot, row * width:row * width + rows], weight[row * triple:(row + 1) * triple],
                           preferred_element_type=jnp.float32)
            result = term if result is None else result + term
        return result

    def back(slot, weight, rows):
        result = None
        for tap in range(9):
            row, col = tap // 3, tap % 3
            start = (8 - tap) * channels
            term = lax.dot_general(stack[slot, row * width:row * width + rows, col * channels:(col + 1) * channels],
                                   weight[start:start + channels], (((1,), (1,)), ((), ())),
                                   preferred_element_type=jnp.float32)
            result = term if result is None else result + term
        return result

    def correlate(which, index, slot, offset, grads):
        for row in range(3):
            start = offset + row * width
            term = lax.dot_general(stack[slot, start:start + pixels], grads, (((0,), (0,)), ((), ())),
                                   preferred_element_type=jnp.float32)
            rows = slice(row * triple, (row + 1) * triple)
            total[which, index, rows] = term
            total_half[which, index, rows] = term.astype(jnp.bfloat16)

    def act(value):
        wide = value.astype(jnp.float32)
        return (wide * jax.nn.sigmoid(wide)).astype(jnp.bfloat16)

    def slope(value):
        wide = value.astype(jnp.float32)
        sigmoid = jax.nn.sigmoid(wide)
        return sigmoid * (1.0 + wide * (1.0 - sigmoid))

    place = lax.broadcasted_iota(jnp.int32, (first_pixels, channels), 0)
    inside = jnp.logical_and(place >= jnp.where(at_top, width, 0),
                             place < jnp.where(at_bottom, width + pixels, first_pixels))

    def trim(value):
        return jnp.where(inside, value, 0.0).astype(jnp.bfloat16)

    grown = slice(width, margin + pixels + width)
    core_rows = slice(margin, margin + pixels)
    kept = slice(width, width + pixels)

    class Tick:
        def __init__(self, tick, which, put, got):
            self.tick, self.which, self.put, self.got = tick, which, put, got

        def field(self, name, rows=core_rows):
            return fields[self.tick, name, rows]

        def weight(self, index):
            return wts.at[self.which, index]

        def advance_first(self):
            fill(ACT_Q, act(fields[self.tick, FWD2]))
            out1 = trim(self.field(FWD1, grown).astype(jnp.float32) + conv(ACT_Q, self.weight(F), first_pixels))
            self.put(FWD1, out1[kept])
            fill(ACT_OUT, act(out1))

        def advance_second(self):
            out2 = self.field(FWD2).astype(jnp.float32) + conv(ACT_OUT, self.weight(G), pixels)
            self.put(FWD2, out2.astype(jnp.bfloat16))

        def fill_returning(self):
            fill(ACT_Y, act(fields[self.tick, RET1]))

        def fill_grad(self):
            fill(GRAD2, fields[self.tick, GRD2])

        def invert_second(self):
            q2 = trim(self.field(RET2, grown).astype(jnp.float32) - conv(ACT_Y, self.weight(G), first_pixels))
            self.put(RET2, q2[kept])
            fill(ACT_IN, act(q2))

        def back_first(self):
            h1 = trim(self.field(GRD1, grown).astype(jnp.float32)
                      + slope(self.field(RET1, grown)) * back(GRAD2, self.weight(G), first_pixels))
            self.put(GRD1, h1[kept])
            fill(BACK1, h1)

        def invert_first(self):
            p2 = self.field(RET1).astype(jnp.float32) - conv(ACT_IN, self.weight(F), pixels)
            self.put(RET1, p2.astype(jnp.bfloat16))

        def back_second(self):
            h2 = (self.field(GRD2).astype(jnp.float32)
                  + slope(self.got(RET2)) * back(BACK1, self.weight(F), pixels))
            self.put(GRD2, h2.astype(jnp.bfloat16))

        def correlate_g(self):
            correlate(self.tick, G, ACT_Y, width, self.field(GRD2))

        def correlate_f(self):
            correlate(self.tick, F, ACT_IN, 0, self.got(GRD1))

    def move(tick, field, target, device):
        return pltpu.make_async_remote_copy(
            src_ref=sent.at[tick, field], dst_ref=target[0], send_sem=(mid_send, end_send)[tick].at[field],
            recv_sem=(mid_recv, end_recv)[tick].at[target[1]], device_id=(device, band), device_id_type=MESH)

    def mid_target(field):
        return fields.at[1, field, inner], field

    def end_target(field):
        return (fwd_out, ret_out, grd_out)[field // 2].at[field % 2], field

    def mid_move(field):
        return move(0, field, mid_target(field), seg + 2 if field < RET1 else seg - 2)

    def turn_move(field):
        return move(0, field, mid_target(field + 2), seg - 1)

    def end_move(field):
        return move(1, field, end_target(field), seg + 2 if field < RET1 else seg - 2)

    def leave_move(field):
        return move(1, field, end_target(field + 2), seg + 1)

    mid_back = jnp.logical_and(even, below)
    mid_on = jnp.logical_and(odd, above)
    end_on = jnp.logical_and(even, above)
    end_back = jnp.logical_and(odd, below)
    leaves = seg == segments - 2

    def send_mid(field):
        if field < RET1:
            pl.when(mid_on)(mid_move(field).start)
            pl.when(last_seg)(turn_move(field).start)
        else:
            pl.when(mid_back)(mid_move(field).start)

    def put_mid(field, value):
        sent[0, field] = value
        if field != GRD1:
            send_mid(field)

        @pl.when(even if field < RET1 else odd)
        def _():
            fields[1, field, core_rows] = value

    def chunk_rows(owner):
        return pl.ds(pl.multiple_of(owner * chunk, chunk), chunk)

    def pair_copy(which, index, target):
        return pltpu.make_async_remote_copy(
            src_ref=total_half.at[which, index, chunk_rows(2 * target + 1 - core)],
            dst_ref=paired.at[which, index, target],
            send_sem=pair_send.at[which, index, target], recv_sem=pair_recv.at[which, index, target],
            device_id=(seg, core_band), device_id_type=MESH)

    def reduce_copy(which, index, step):
        return pltpu.make_async_remote_copy(
            src_ref=reduced.at[which, index, step - 1], dst_ref=partial.at[which, index, step - 1],
            send_sem=red_send.at[which, index, step - 1], recv_sem=red_recv.at[which, index, step - 1],
            device_id=(seg, 2 * lax.rem(group + step, groups) + core), device_id_type=MESH)

    def ship_copy(index):
        return pltpu.make_async_remote_copy(
            src_ref=ship_src.at[index], dst_ref=ship_dst.at[index],
            send_sem=ship_send.at[index], recv_sem=ship_recv.at[index],
            device_id=(other_seg, band), device_id_type=MESH)

    def start_sums(which, index):
        for target in range(groups):
            pair_copy(which, index, target).start()

    def pair_sum(which, index, target):
        return total[which, index, chunk_rows(2 * target + core)] + paired[which, index, target].astype(jnp.float32)

    def pass_sums(which, index):
        for target in range(groups):
            pair_copy(which, index, target).wait_recv()
        for step in range(1, groups):
            reduced[which, index, step - 1] = pair_sum(which, index, lax.rem(group + step, groups)).astype(jnp.bfloat16)
            reduce_copy(which, index, step).start()

    def finish_sums(which, index):
        value = pair_sum(which, index, group)
        for step in range(1, groups):
            reduce_copy(which, index, step).wait_recv()
            value = value + partial[which, index, step - 1].astype(jnp.float32)
        return value

    def keep_sums(index):
        owned[index] = finish_sums(OWN, index)

    def ship_sums(index):
        ship_src[index] = finish_sums(OTHER, index).astype(jnp.bfloat16)
        ship_copy(index).start()

    def close_sums(index):
        ship_copy(index).wait_recv()
        wgrad_out[index] = owned[index] + ship_dst[index].astype(jnp.float32)

    first = Tick(0, OWN, put_mid, lambda field: sent[0, field])
    load(RET1).wait()
    load(GRD2).wait()
    load_weights(G).wait()
    load(RET2).wait()
    load(GRD1).wait()
    load_weights(F).wait()
    load(FWD2).wait()
    load(FWD1).wait()
    neighbours = below.astype(jnp.int32) + above.astype(jnp.int32)
    pl.semaphore_wait(barrier, bands + neighbours)
    for field in (RET1, GRD2, RET2, GRD1, FWD2, FWD1):
        send_halo(0, field)
    for index in (G, F):
        for part in range(pieces):
            w_across(index, part).start()

    take_halo(0, RET1)
    first.fill_returning()
    take_halo(0, RET2)
    first.invert_second()
    take_halo(0, GRD2)
    first.fill_grad()
    take_halo(0, GRD1)
    first.back_first()
    first.invert_first()
    first.back_second()
    send_mid(GRD1)

    @pl.when(odd)
    def _():
        for field in (RET1, GRD2, RET2, GRD1):
            send_halo(1, field)

    for part in range(pieces - 1):
        spread_weights(G, part)
    take_halo(0, FWD2)
    take_halo(0, FWD1)
    first.advance_first()
    first.advance_second()

    @pl.when(even)
    def _():
        for field in (FWD2, FWD1):
            send_halo(1, field)

    spread_weights(G, pieces - 1)
    first.correlate_g()
    start_sums(OWN, G)
    first.correlate_f()
    start_sums(OWN, F)
    for part in range(pieces):
        pass_weights(G, part)
    for part in range(pieces - 1):
        spread_weights(F, part)

    @pl.when(odd)
    def _():
        def put(field, value):
            if field < RET1:
                fwd_out[field] = value
            else:
                sent[1, field] = value
                pl.when(end_back)(end_move(field).start)

        last = Tick(1, OTHER, put, lambda field: sent[1, field])
        take_halo(1, RET1)
        last.fill_returning()
        take_halo(1, GRD2)
        last.fill_grad()
        take_halo(1, RET2)
        take_halo(1, GRD1)
        take_weights(G)
        last.invert_second()
        last.back_first()
        last.correlate_g()
        start_sums(OTHER, G)
        last.correlate_f()
        start_sums(OTHER, F)
        spread_weights(F, pieces - 1)
        for part in range(pieces):
            pass_weights(F, part)
        pass_sums(OTHER, G)
        pass_sums(OTHER, F)
        take_weights(F)
        last.invert_first()
        last.back_second()
        pass_sums(OWN, G)
        pass_sums(OWN, F)

        for field in (FWD2, FWD1):
            pl.when(below)(mid_move(field).wait_recv)
        pl.when(seg == 1)(edge(0).wait)
        for field in (FWD2, FWD1):
            send_halo(1, field)
        for field in (FWD2, FWD1):
            take_halo(1, field)
        last.advance_first()
        last.advance_second()
        ship_sums(G)
        ship_sums(F)
        keep_sums(G)
        keep_sums(F)

    @pl.when(even)
    def _():
        def put(field, value):
            if field < RET1:
                sent[1, field] = value
                pl.when(end_on)(end_move(field).start)
                pl.when(leaves)(leave_move(field).start)
            else:
                (ret_out, grd_out)[field // 2 - 1][field % 2] = value

        last = Tick(1, OTHER, put, lambda field: (ret_out, grd_out)[field // 2 - 1][field % 2])
        spread_weights(F, pieces - 1)
        for part in range(pieces):
            pass_weights(F, part)
        pass_sums(OWN, G)
        pass_sums(OWN, F)
        take_weights(F)
        take_weights(G)
        for field in (FWD2, FWD1):
            take_halo(1, field)
        last.advance_first()
        last.advance_second()

        def arrive(field):
            if field < GRD1:
                mid_move(field).wait_recv()
            else:
                pl.when(above)(mid_move(field).wait_recv)
                if field == GRD2:
                    pl.when(leaves)(edge(2).wait)
            send_halo(1, field)

        arrive(RET2)
        arrive(RET1)
        take_halo(1, RET1)
        last.fill_returning()
        take_halo(1, RET2)
        last.invert_second()
        arrive(GRD2)
        keep_sums(G)
        keep_sums(F)
        take_halo(1, GRD2)
        last.correlate_g()
        start_sums(OTHER, G)
        last.fill_grad()
        arrive(GRD1)
        take_halo(1, GRD1)
        pass_sums(OTHER, G)
        last.back_first()
        last.correlate_f()
        start_sums(OTHER, F)
        last.invert_first()
        pass_sums(OTHER, F)
        last.back_second()
        ship_sums(G)
        ship_sums(F)

    close_sums(G)
    close_sums(F)

    pl.when(first_seg)(edge(1).wait)
    pl.when(last_seg)(edge(3).wait)
    for field in (FWD1, FWD2):
        pl.when(jnp.logical_and(even, below))(end_move(field).wait_recv)
        pl.when(last_seg)(end_move(field + 2).wait_recv)
    for field in (RET1, RET2, GRD1, GRD2):
        pl.when(jnp.logical_and(odd, above))(end_move(field).wait_recv)

    for field in range(6):
        for tick in range(2):
            pl.when(jnp.logical_not(at_top))(halo_copy(tick, field, 0).wait_send)
            pl.when(jnp.logical_not(at_bottom))(halo_copy(tick, field, 1).wait_send)
        if field < RET1:
            pl.when(mid_on)(mid_move(field).wait_send)
            pl.when(last_seg)(turn_move(field).wait_send)
            pl.when(end_on)(end_move(field).wait_send)
            pl.when(leaves)(leave_move(field).wait_send)
        else:
            pl.when(mid_back)(mid_move(field).wait_send)
            pl.when(end_back)(end_move(field).wait_send)
    for index in range(2):
        for part in range(pieces):
            w_across(index, part).wait_send()
            for step in range(1, groups):
                w_group(index, part, step).wait_send()
            for step in range(groups):
                w_core(index, part, step).wait_send()
        for which in range(2):
            for target in range(groups):
                pair_copy(which, index, target).wait_send()
            for step in range(1, groups):
                reduce_copy(which, index, step).wait_send()
        ship_copy(index).wait_send()


def store(*refs):
    count = (len(refs) - 2) // 3
    sources, targets, held = refs[:count], refs[count:2 * count], refs[2 * count:3 * count]
    load_sem, store_sem = refs[3 * count:]
    loads = [pltpu.make_async_copy(sources[i], held[i], load_sem.at[i]) for i in range(count)]
    stores = [pltpu.make_async_copy(held[i], targets[i], store_sem.at[i]) for i in range(count)]
    for load in loads:
        load.start()
    for load, out in zip(loads, stores):
        load.wait()
        out.start()
    for out in stores:
        out.wait()


def local(forward_state, returning_state, returning_grad, weights, fresh_input, loss_grad):
    segments, bands = lax.axis_size("segment"), lax.axis_size("band")
    _, _, rows, width, channels = forward_state.shape
    pixels = rows * width
    taps = weights.shape[2]
    chunk = taps // bands
    groups = bands // 2
    pieces = 2 if chunk % 32 == 0 else 1
    assert fresh_input.shape[0] == 2 and segments % 2 == 0 and bands % 2 == 0 and rows >= 2
    bf16, f32 = jnp.bfloat16, jnp.float32
    pair = jax.ShapeDtypeStruct((2, pixels, channels), bf16)
    dma = pltpu.SemaphoreType.DMA
    flat = lambda x: x.reshape(x.shape[:-3] + (pixels, channels))
    vmem = pl.BlockSpec(memory_space=pltpu.VMEM)
    outs = pl.pallas_call(
        functools.partial(kernel, segments, bands, width, pieces),
        out_shape=(pair, pair, pair, jax.ShapeDtypeStruct((2, chunk, channels), f32)),
        in_specs=[pl.BlockSpec(memory_space=pl.ANY)] * 6,
        out_specs=(vmem,) * 4,
        scratch_shapes=[
            pltpu.VMEM((2, 6, pixels + 4 * width, channels), bf16),
            pltpu.VMEM((2, 2, taps, channels), bf16),
            pltpu.VMEM((6, pixels + 4 * width, 3 * channels), bf16),
            pltpu.VMEM((2, 6, pixels, channels), bf16),
            pltpu.VMEM((2, 2, taps, channels), f32),
            pltpu.VMEM((2, 2, taps, channels), bf16),
            pltpu.VMEM((2, 2, groups, chunk, channels), bf16),
            pltpu.VMEM((2, 2, groups - 1, chunk, channels), bf16),
            pltpu.VMEM((2, 2, groups - 1, chunk, channels), bf16),
            pltpu.VMEM((2, chunk, channels), f32),
            pltpu.VMEM((2, chunk, channels), bf16),
            pltpu.VMEM((2, chunk, channels), bf16),
            dma((6,)),
            dma((2,)),
            dma((4,)),
            dma((2, 6, 2)),
            dma((2, 6, 2)),
            dma((6,)),
            dma((6,)),
            dma((6,)),
            dma((6,)),
            dma((2, pieces)),
            dma((2, pieces)),
            dma((2, pieces, groups - 1)),
            dma((2, pieces, groups - 1)),
            dma((2, pieces, groups)),
            dma((2, pieces, groups)),
            dma((2, 2, groups)),
            dma((2, 2, groups)),
            dma((2, 2, groups - 1)),
            dma((2, 2, groups - 1)),
            dma((2,)),
            dma((2,)),
        ],
        compiler_params=pltpu.CompilerParams(
            collective_id=0, has_side_effects=True, vmem_limit_bytes=60 * 2**20),
    )(flat(forward_state[0]), flat(returning_state[0]), flat(returning_grad[0]), weights[0],
      flat(fresh_input), flat(loss_grad))
    outs = pl.pallas_call(
        store,
        out_shape=tuple(jax.ShapeDtypeStruct(o.shape, o.dtype) for o in outs),
        in_specs=[pl.BlockSpec(memory_space=pl.ANY)] * 4,
        out_specs=(pl.BlockSpec(memory_space=pl.ANY),) * 4,
        scratch_shapes=[pltpu.VMEM(o.shape, o.dtype) for o in outs] + [dma((4,)), dma((4,))],
    )(*outs)
    shape = forward_state.shape
    return tuple(o.reshape(shape) for o in outs[:3]) + (outs[3][None],)


def solution(mesh):
    pair = P("segment", None, "band", None, None)
    whole = P(None, None, "band", None, None)
    return jax.shard_map(
        local,
        mesh=mesh,
        in_specs=(pair, pair, pair, P("segment", None, None, None), whole, whole),
        out_specs=(pair, pair, pair, P("segment", None, "band", None)),
        check_vma=False,
    )
```

```python
import functools

import jax
import jax.numpy as jnp
from jax import lax
from jax.experimental import pallas as pl
from jax.experimental.pallas import tpu as pltpu
from jax.sharding import PartitionSpec as P

MESH = pl.DeviceIdType.MESH
ACT_Q, ACT_OUT, ACT_Y, GRAD2, ACT_IN, BACK1 = range(6)
FWD1, FWD2, RET1, RET2, GRD1, GRD2 = range(6)
F, G = 0, 1
OWN, OTHER = 0, 1
TAKES = {ACT_Q: FWD2, ACT_Y: RET1, GRAD2: GRD2}
DEPTH = {FWD1: 1, FWD2: 2, RET1: 2, RET2: 1, GRD1: 1, GRD2: 2}


def kernel(segments, bands, width, pieces, fwd_in, ret_in, grd_in, weights_in, fresh_in, loss_in,
           fwd_out, ret_out, grd_out, wgrad_out,
           fields, wts, stack, sent, total, total_half, paired, reduced, partial, owned, ship_src, ship_dst,
           in_sem, w_sem, edge_sem, halo_send, halo_recv, mid_send, mid_recv, end_send, end_recv,
           wy_send, wy_recv, wx_send, wx_recv, wc_send, wc_recv,
           pair_send, pair_recv, red_send, red_recv, ship_send, ship_recv):
    seg = lax.axis_index("segment")
    band = lax.axis_index("band")
    pixels = sent.shape[2]
    channels = sent.shape[3]
    triple = 3 * channels
    chunk = partial.shape[3]
    margin = 2 * width
    inner = pl.ds(margin, pixels)
    first_pixels = pixels + 2 * width
    parity = lax.rem(seg, 2)
    even, odd = parity == 0, parity == 1
    other_seg = seg + 1 - 2 * parity
    first_seg, last_seg = seg == 0, seg == segments - 1
    below, above = seg >= 2, seg < segments - 2
    groups = bands // 2
    core, group = lax.rem(band, 2), band // 2
    core_band = band + 1 - 2 * core
    at_top, at_bottom = band == 0, band == bands - 1

    sources = {FWD1: fwd_in.at[0], FWD2: fwd_in.at[1], RET1: ret_in.at[0], RET2: ret_in.at[1],
               GRD1: grd_in.at[0], GRD2: grd_in.at[1]}

    def load(field):
        return pltpu.make_async_copy(sources[field], fields.at[0, field, inner], in_sem.at[field])

    def load_weights(index):
        return pltpu.make_async_copy(weights_in.at[index], wts.at[OWN, index], w_sem.at[index])

    load(RET1).start()
    load(GRD2).start()
    load_weights(G).start()
    load(RET2).start()
    load(GRD1).start()
    load_weights(F).start()
    load(FWD2).start()
    load(FWD1).start()

    barrier = pltpu.get_barrier_semaphore()
    for step in range(1, bands):
        pl.semaphore_signal(barrier, inc=1, device_id=(seg, lax.rem(band + step, bands)), device_id_type=MESH)
    pl.semaphore_signal(barrier, inc=1, device_id=(other_seg, band), device_id_type=MESH)

    @pl.when(below)
    def _():
        pl.semaphore_signal(barrier, inc=1, device_id=(seg - 2, band), device_id_type=MESH)

    @pl.when(above)
    def _():
        pl.semaphore_signal(barrier, inc=1, device_id=(seg + 2, band), device_id_type=MESH)

    def edge(which):
        return (
            pltpu.make_async_copy(fresh_in.at[0], fields.at[1, pl.ds(FWD1, 2), inner], edge_sem.at[0]),
            pltpu.make_async_copy(fresh_in.at[1], fwd_out, edge_sem.at[1]),
            pltpu.make_async_copy(loss_in.at[0], fields.at[1, pl.ds(GRD1, 2), inner], edge_sem.at[2]),
            pltpu.make_async_copy(loss_in.at[1], grd_out, edge_sem.at[3]),
        )[which]

    edge_places = (seg == 1, first_seg, seg == segments - 2, last_seg)
    for which in range(4):
        pl.when(edge_places[which])(edge(which).start)

    @pl.when(at_top)
    def _():
        fields[:, :, 0:margin] = jnp.zeros((2, 6, margin, channels), jnp.bfloat16)

    @pl.when(at_bottom)
    def _():
        fields[:, :, margin + pixels:] = jnp.zeros((2, 6, margin, channels), jnp.bfloat16)

    def halo_copy(tick, field, side):
        size = DEPTH[field] * width
        if side == 0:
            source, target = margin, margin + pixels
        else:
            source, target = margin + pixels - size, margin - size
        return pltpu.make_async_remote_copy(
            src_ref=fields.at[tick, field, pl.ds(source, size)], dst_ref=fields.at[tick, field, pl.ds(target, size)],
            send_sem=halo_send.at[tick, field, side], recv_sem=halo_recv.at[tick, field, 1 - side],
            device_id=(seg, band - 1 if side == 0 else band + 1), device_id_type=MESH)

    def send_halo(tick, field):
        pl.when(jnp.logical_not(at_top))(halo_copy(tick, field, 0).start)
        pl.when(jnp.logical_not(at_bottom))(halo_copy(tick, field, 1).start)

    def take_halo(tick, field):
        pl.when(jnp.logical_not(at_top))(halo_copy(tick, field, 1).wait_recv)
        pl.when(jnp.logical_not(at_bottom))(halo_copy(tick, field, 0).wait_recv)

    piece = chunk // pieces

    def w_rows(owner, part):
        return pl.ds(pl.multiple_of(owner * chunk + part * piece, piece), piece)

    def w_across(index, part):
        return pltpu.make_async_remote_copy(
            src_ref=wts.at[OWN, index, w_rows(band, part)], dst_ref=wts.at[OTHER, index, w_rows(band, part)],
            send_sem=wy_send.at[index, part], recv_sem=wy_recv.at[index, part],
            device_id=(other_seg, band), device_id_type=MESH)

    def w_group(index, part, step):
        rows = w_rows(band, part)
        return pltpu.make_async_remote_copy(
            src_ref=wts.at[OTHER, index, rows], dst_ref=wts.at[OTHER, index, rows],
            send_sem=wx_send.at[index, part, step - 1], recv_sem=wx_recv.at[index, part, step - 1],
            device_id=(seg, 2 * lax.rem(group + step, groups) + core), device_id_type=MESH)

    def w_core(index, part, step):
        rows = w_rows(2 * lax.rem(group + groups - step, groups) + core, part)
        return pltpu.make_async_remote_copy(
            src_ref=wts.at[OTHER, index, rows], dst_ref=wts.at[OTHER, index, rows],
            send_sem=wc_send.at[index, part, step], recv_sem=wc_recv.at[index, part, step],
            device_id=(seg, core_band), device_id_type=MESH)

    def w_direct(index, part, step):
        rows = w_rows(2 * lax.rem(group + groups - step, groups) + core, part)
        return pltpu.make_async_remote_copy(
            src_ref=wts.at[OWN, index, rows], dst_ref=wts.at[OTHER, index, rows],
            send_sem=wx_send.at[index, part, step - 1], recv_sem=wx_recv.at[index, part, step - 1],
            device_id=(other_seg, band), device_id_type=MESH)

    straight = jnp.logical_and(above, other_seg < segments - 2) if groups == 2 else jnp.bool_(False)

    def start_weights(index):
        for part in range(pieces):
            w_across(index, part).start()
            if index == F:
                for step in range(1, groups):
                    pl.when(straight)(w_direct(index, part, step).start)

    def spread_weights(index, part):
        w_across(index, part).wait_recv()
        for step in range(1, groups):
            if index == F:
                pl.when(jnp.logical_not(straight))(w_group(index, part, step).start)
            else:
                w_group(index, part, step).start()
        w_core(index, part, 0).start()

    def pass_weights(index, part):
        for step in range(1, groups):
            w_group(index, part, step).wait_recv()
            w_core(index, part, step).start()

    def take_weights(index):
        for part in range(pieces):
            for step in range(groups):
                w_core(index, part, step).wait_recv()

    def fill(slot, value, start=0):
        rows = value.shape[0]
        column = lax.rem(lax.broadcasted_iota(jnp.int32, (rows, channels), 0), width)
        wide = value.astype(jnp.float32)
        left = jnp.where(column == 0, 0.0, pltpu.roll(wide, 1, 0))
        right = jnp.where(column == width - 1, 0.0, pltpu.roll(wide, rows - 1, 0))
        stack[slot, start:start + rows, 0:channels] = left.astype(jnp.bfloat16)
        stack[slot, start:start + rows, channels:2 * channels] = value
        stack[slot, start:start + rows, 2 * channels:triple] = right.astype(jnp.bfloat16)

    def conv(slot, weight, rows):
        result = None
        for row in range(3):
            term = jnp.dot(stack[slot, row * width:row * width + rows], weight[row * triple:(row + 1) * triple],
                           preferred_element_type=jnp.float32)
            result = term if result is None else result + term
        return result

    def back(slot, weight, rows):
        result = None
        for tap in range(9):
            row, col = tap // 3, tap % 3
            start = (8 - tap) * channels
            term = lax.dot_general(stack[slot, row * width:row * width + rows, col * channels:(col + 1) * channels],
                                   weight[start:start + channels], (((1,), (1,)), ((), ())),
                                   preferred_element_type=jnp.float32)
            result = term if result is None else result + term
        return result

    def correlate(which, index, slot, offset, grads):
        for row in range(3):
            start = offset + row * width
            term = lax.dot_general(stack[slot, start:start + pixels], grads, (((0,), (0,)), ((), ())),
                                   preferred_element_type=jnp.float32)
            rows = slice(row * triple, (row + 1) * triple)
            total[which, index, rows] = term
            total_half[which, index, rows] = term.astype(jnp.bfloat16)

    def act(value):
        wide = value.astype(jnp.float32)
        return (wide * jax.nn.sigmoid(wide)).astype(jnp.bfloat16)

    def slope(value):
        wide = value.astype(jnp.float32)
        sigmoid = jax.nn.sigmoid(wide)
        return sigmoid * (1.0 + wide * (1.0 - sigmoid))

    place = lax.broadcasted_iota(jnp.int32, (first_pixels, channels), 0)
    inside = jnp.logical_and(place >= jnp.where(at_top, width, 0),
                             place < jnp.where(at_bottom, width + pixels, first_pixels))

    def trim(value):
        return jnp.where(inside, value, 0.0).astype(jnp.bfloat16)

    grown = slice(width, margin + pixels + width)
    core_rows = slice(margin, margin + pixels)
    kept = slice(width, width + pixels)

    class Tick:
        def __init__(self, tick, which, put, got):
            self.tick, self.which, self.put, self.got = tick, which, put, got

        def field(self, name, rows=core_rows):
            return fields[self.tick, name, rows]

        def weight(self, index):
            return wts.at[self.which, index]

        def advance_first(self):
            out1 = trim(self.field(FWD1, grown).astype(jnp.float32) + conv(ACT_Q, self.weight(F), first_pixels))
            self.put(FWD1, out1[kept])
            fill(ACT_OUT, act(out1))

        def advance_second(self):
            out2 = self.field(FWD2).astype(jnp.float32) + conv(ACT_OUT, self.weight(G), pixels)
            self.put(FWD2, out2.astype(jnp.bfloat16))

        def fill_inner(self, slot):
            value = self.field(TAKES[slot])
            fill(slot, value if slot == GRAD2 else act(value), margin)

        def fill_margins(self, slot):
            for start in (0, margin + pixels):
                value = fields[self.tick, TAKES[slot], start:start + margin]
                fill(slot, value if slot == GRAD2 else act(value), start)

        def invert_second(self):
            q2 = trim(self.field(RET2, grown).astype(jnp.float32) - conv(ACT_Y, self.weight(G), first_pixels))
            self.put(RET2, q2[kept])
            fill(ACT_IN, act(q2))

        def back_first(self):
            h1 = trim(self.field(GRD1, grown).astype(jnp.float32)
                      + slope(self.field(RET1, grown)) * back(GRAD2, self.weight(G), first_pixels))
            self.put(GRD1, h1[kept])
            fill(BACK1, h1)

        def invert_first(self):
            p2 = self.field(RET1).astype(jnp.float32) - conv(ACT_IN, self.weight(F), pixels)
            self.put(RET1, p2.astype(jnp.bfloat16))

        def back_second(self):
            h2 = (self.field(GRD2).astype(jnp.float32)
                  + slope(self.got(RET2)) * back(BACK1, self.weight(F), pixels))
            self.put(GRD2, h2.astype(jnp.bfloat16))

        def correlate_g(self):
            correlate(self.tick, G, ACT_Y, width, self.field(GRD2))

        def correlate_f(self):
            correlate(self.tick, F, ACT_IN, 0, self.got(GRD1))

    def move(tick, field, target, device):
        return pltpu.make_async_remote_copy(
            src_ref=sent.at[tick, field], dst_ref=target[0], send_sem=(mid_send, end_send)[tick].at[field],
            recv_sem=(mid_recv, end_recv)[tick].at[target[1]], device_id=(device, band), device_id_type=MESH)

    def mid_target(field):
        return fields.at[1, field, inner], field

    def end_target(field):
        return (fwd_out, ret_out, grd_out)[field // 2].at[field % 2], field

    def mid_move(field):
        return move(0, field, mid_target(field), seg + 2 if field < RET1 else seg - 2)

    def turn_move(field):
        return move(0, field, mid_target(field + 2), seg - 1)

    def end_move(field):
        return move(1, field, end_target(field), seg + 2 if field < RET1 else seg - 2)

    def leave_move(field):
        return move(1, field, end_target(field + 2), seg + 1)

    mid_back = jnp.logical_and(even, below)
    mid_on = jnp.logical_and(odd, above)
    end_on = jnp.logical_and(even, above)
    end_back = jnp.logical_and(odd, below)
    leaves = seg == segments - 2

    def send_mid(field):
        if field < RET1:
            pl.when(mid_on)(mid_move(field).start)
            pl.when(last_seg)(turn_move(field).start)
        else:
            pl.when(mid_back)(mid_move(field).start)

    def put_mid(field, value):
        sent[0, field] = value
        if field != GRD1:
            send_mid(field)

        @pl.when(even if field < RET1 else odd)
        def _():
            fields[1, field, core_rows] = value

    def chunk_rows(owner):
        return pl.ds(pl.multiple_of(owner * chunk, chunk), chunk)

    def pair_copy(which, index, target):
        return pltpu.make_async_remote_copy(
            src_ref=total_half.at[which, index, chunk_rows(2 * target + 1 - core)],
            dst_ref=paired.at[which, index, target],
            send_sem=pair_send.at[which, index, target], recv_sem=pair_recv.at[which, index, target],
            device_id=(seg, core_band), device_id_type=MESH)

    def reduce_copy(which, index, part, step):
        rows = pl.ds(part * piece, piece)
        return pltpu.make_async_remote_copy(
            src_ref=reduced.at[which, index, step - 1, rows], dst_ref=partial.at[which, index, step - 1, rows],
            send_sem=red_send.at[which, index, part, step - 1], recv_sem=red_recv.at[which, index, part, step - 1],
            device_id=(seg, 2 * lax.rem(group + step, groups) + core), device_id_type=MESH)

    def ship_copy(index, part):
        rows = pl.ds(part * piece, piece)
        return pltpu.make_async_remote_copy(
            src_ref=ship_src.at[index, rows], dst_ref=ship_dst.at[index, rows],
            send_sem=ship_send.at[index, part], recv_sem=ship_recv.at[index, part],
            device_id=(other_seg, band), device_id_type=MESH)

    def start_sums(which, index):
        for target in range(groups):
            pair_copy(which, index, target).start()

    def pair_sum(which, index, target, part):
        rows = pl.ds(part * piece, piece)
        return (total[which, index, w_rows(2 * target + core, part)]
                + paired[which, index, target, rows].astype(jnp.float32))

    def pass_sums(which, index):
        for target in range(groups):
            pair_copy(which, index, target).wait_recv()
        for part in range(pieces):
            rows = pl.ds(part * piece, piece)
            for step in range(1, groups):
                value = pair_sum(which, index, lax.rem(group + step, groups), part)
                reduced[which, index, step - 1, rows] = value.astype(jnp.bfloat16)
                reduce_copy(which, index, part, step).start()

    def finish_sums(which, index, part):
        value = pair_sum(which, index, group, part)
        for step in range(1, groups):
            reduce_copy(which, index, part, step).wait_recv()
            value = value + partial[which, index, step - 1, pl.ds(part * piece, piece)].astype(jnp.float32)
        return value

    def keep_sums(index):
        for part in range(pieces):
            owned[index, pl.ds(part * piece, piece)] = finish_sums(OWN, index, part)

    def ship_sums(index):
        for part in range(pieces):
            ship_src[index, pl.ds(part * piece, piece)] = finish_sums(OTHER, index, part).astype(jnp.bfloat16)
            ship_copy(index, part).start()

    def close_sums(index):
        for part in range(pieces):
            rows = pl.ds(part * piece, piece)
            ship_copy(index, part).wait_recv()
            wgrad_out[index, rows] = owned[index, rows] + ship_dst[index, rows].astype(jnp.float32)

    first = Tick(0, OWN, put_mid, lambda field: sent[0, field])
    load(RET1).wait()
    first.fill_inner(ACT_Y)
    load(GRD2).wait()
    first.fill_inner(GRAD2)
    load(FWD2).wait()
    first.fill_inner(ACT_Q)
    load(RET2).wait()
    load(GRD1).wait()
    load(FWD1).wait()
    load_weights(G).wait()
    load_weights(F).wait()
    neighbours = below.astype(jnp.int32) + above.astype(jnp.int32)
    pl.semaphore_wait(barrier, bands + neighbours)
    for field in (RET1, RET2, GRD2, GRD1, FWD2, FWD1):
        send_halo(0, field)
    start_weights(G)
    start_weights(F)

    take_halo(0, RET1)
    first.fill_margins(ACT_Y)
    take_halo(0, RET2)
    first.invert_second()
    take_halo(0, GRD2)
    first.fill_margins(GRAD2)
    take_halo(0, GRD1)
    first.back_first()
    spread_weights(G, 0)
    first.invert_first()
    first.back_second()
    send_mid(GRD1)

    @pl.when(odd)
    def _():
        for field in (RET1, RET2, GRD2, GRD1):
            send_halo(1, field)

    for part in range(1, pieces):
        spread_weights(G, part)
    take_halo(0, FWD2)
    first.fill_margins(ACT_Q)
    take_halo(0, FWD1)
    first.advance_first()
    first.advance_second()

    @pl.when(even)
    def _():
        for field in (FWD2, FWD1):
            send_halo(1, field)

    first.correlate_g()
    start_sums(OWN, G)
    for part in range(pieces):
        pass_weights(G, part)
    first.correlate_f()
    start_sums(OWN, F)
    pass_sums(OWN, G)

    @pl.when(odd)
    def _():
        def put(field, value):
            if field < RET1:
                fwd_out[field] = value
            else:
                sent[1, field] = value
                pl.when(end_back)(end_move(field).start)

        last = Tick(1, OTHER, put, lambda field: sent[1, field])
        last.fill_inner(ACT_Y)
        last.fill_inner(GRAD2)
        take_halo(1, RET1)
        last.fill_margins(ACT_Y)
        take_halo(1, GRD2)
        last.fill_margins(GRAD2)
        take_halo(1, RET2)
        take_halo(1, GRD1)
        take_weights(G)
        last.invert_second()
        last.back_first()
        last.correlate_g()
        start_sums(OTHER, G)
        for part in range(pieces):
            spread_weights(F, part)
        last.correlate_f()
        start_sums(OTHER, F)
        pass_sums(OTHER, G)
        for part in range(pieces):
            pass_weights(F, part)
        pass_sums(OTHER, F)
        take_weights(F)
        last.invert_first()
        last.back_second()
        pass_sums(OWN, F)
        for field in (FWD2, FWD1):
            pl.when(below)(mid_move(field).wait_recv)
        pl.when(seg == 1)(edge(0).wait)
        for field in (FWD2, FWD1):
            send_halo(1, field)
        last.fill_inner(ACT_Q)
        keep_sums(G)
        ship_sums(G)
        for field in (FWD2, FWD1):
            take_halo(1, field)
        last.fill_margins(ACT_Q)
        last.advance_first()
        last.advance_second()
        ship_sums(F)
        keep_sums(F)

    @pl.when(even)
    def _():
        def put(field, value):
            if field < RET1:
                sent[1, field] = value
                pl.when(end_on)(end_move(field).start)
                pl.when(leaves)(leave_move(field).start)
            else:
                (ret_out, grd_out)[field // 2 - 1][field % 2] = value

        last = Tick(1, OTHER, put, lambda field: (ret_out, grd_out)[field // 2 - 1][field % 2])

        def arrive(field):
            if field < GRD1:
                mid_move(field).wait_recv()
            else:
                pl.when(above)(mid_move(field).wait_recv)
                if field == GRD2:
                    pl.when(leaves)(edge(2).wait)
            send_halo(1, field)

        for part in range(pieces):
            spread_weights(F, part)
        last.fill_inner(ACT_Q)
        arrive(RET2)
        arrive(RET1)
        last.fill_inner(ACT_Y)
        pass_sums(OWN, F)
        for part in range(pieces):
            pass_weights(F, part)
        take_weights(G)
        take_halo(1, RET1)
        last.fill_margins(ACT_Y)
        take_halo(1, RET2)
        last.invert_second()
        for field in (FWD2, FWD1):
            take_halo(1, field)
        last.fill_margins(ACT_Q)
        take_weights(F)
        last.advance_first()
        arrive(GRD2)
        last.advance_second()
        last.correlate_g()
        start_sums(OTHER, G)
        last.fill_inner(GRAD2)
        take_halo(1, GRD2)
        last.fill_margins(GRAD2)
        arrive(GRD1)
        pass_sums(OTHER, G)
        last.invert_first()
        take_halo(1, GRD1)
        last.back_first()
        last.correlate_f()
        start_sums(OTHER, F)
        last.back_second()
        pass_sums(OTHER, F)
        keep_sums(G)
        keep_sums(F)
        ship_sums(G)
        ship_sums(F)

    close_sums(G)
    close_sums(F)

    pl.when(first_seg)(edge(1).wait)
    pl.when(last_seg)(edge(3).wait)
    for field in (FWD1, FWD2):
        pl.when(jnp.logical_and(even, below))(end_move(field).wait_recv)
        pl.when(last_seg)(end_move(field + 2).wait_recv)
    for field in (RET1, RET2, GRD1, GRD2):
        pl.when(jnp.logical_and(odd, above))(end_move(field).wait_recv)

    for field in range(6):
        for tick in range(2):
            pl.when(jnp.logical_not(at_top))(halo_copy(tick, field, 0).wait_send)
            pl.when(jnp.logical_not(at_bottom))(halo_copy(tick, field, 1).wait_send)
        if field < RET1:
            pl.when(mid_on)(mid_move(field).wait_send)
            pl.when(last_seg)(turn_move(field).wait_send)
            pl.when(end_on)(end_move(field).wait_send)
            pl.when(leaves)(leave_move(field).wait_send)
        else:
            pl.when(mid_back)(mid_move(field).wait_send)
            pl.when(end_back)(end_move(field).wait_send)
    for index in range(2):
        for part in range(pieces):
            w_across(index, part).wait_send()
            for step in range(1, groups):
                w_group(index, part, step).wait_send()
            for step in range(groups):
                w_core(index, part, step).wait_send()
        for which in range(2):
            for target in range(groups):
                pair_copy(which, index, target).wait_send()
            for part in range(pieces):
                for step in range(1, groups):
                    reduce_copy(which, index, part, step).wait_send()
        for part in range(pieces):
            ship_copy(index, part).wait_send()


def store(*refs):
    count = (len(refs) - 2) // 3
    sources, targets, held = refs[:count], refs[count:2 * count], refs[2 * count:3 * count]
    load_sem, store_sem = refs[3 * count:]
    loads = [pltpu.make_async_copy(sources[i], held[i], load_sem.at[i]) for i in range(count)]
    stores = [pltpu.make_async_copy(held[i], targets[i], store_sem.at[i]) for i in range(count)]
    for load in loads:
        load.start()
    for load, out in zip(loads, stores):
        load.wait()
        out.start()
    for out in stores:
        out.wait()


def local(forward_state, returning_state, returning_grad, weights, fresh_input, loss_grad):
    segments, bands = lax.axis_size("segment"), lax.axis_size("band")
    _, _, rows, width, channels = forward_state.shape
    pixels = rows * width
    taps = weights.shape[2]
    chunk = taps // bands
    groups = bands // 2
    pieces = 2 if chunk % 32 == 0 else 1
    assert fresh_input.shape[0] == 2 and segments % 2 == 0 and bands % 2 == 0 and rows >= 2
    bf16, f32 = jnp.bfloat16, jnp.float32
    pair = jax.ShapeDtypeStruct((2, pixels, channels), bf16)
    dma = pltpu.SemaphoreType.DMA
    flat = lambda x: x.reshape(x.shape[:-3] + (pixels, channels))
    vmem = pl.BlockSpec(memory_space=pltpu.VMEM)
    outs = pl.pallas_call(
        functools.partial(kernel, segments, bands, width, pieces),
        out_shape=(pair, pair, pair, jax.ShapeDtypeStruct((2, chunk, channels), f32)),
        in_specs=[pl.BlockSpec(memory_space=pl.ANY)] * 6,
        out_specs=(vmem,) * 4,
        scratch_shapes=[
            pltpu.VMEM((2, 6, pixels + 4 * width, channels), bf16),
            pltpu.VMEM((2, 2, taps, channels), bf16),
            pltpu.VMEM((6, pixels + 4 * width, 3 * channels), bf16),
            pltpu.VMEM((2, 6, pixels, channels), bf16),
            pltpu.VMEM((2, 2, taps, channels), f32),
            pltpu.VMEM((2, 2, taps, channels), bf16),
            pltpu.VMEM((2, 2, groups, chunk, channels), bf16),
            pltpu.VMEM((2, 2, groups - 1, chunk, channels), bf16),
            pltpu.VMEM((2, 2, groups - 1, chunk, channels), bf16),
            pltpu.VMEM((2, chunk, channels), f32),
            pltpu.VMEM((2, chunk, channels), bf16),
            pltpu.VMEM((2, chunk, channels), bf16),
            dma((6,)),
            dma((2,)),
            dma((4,)),
            dma((2, 6, 2)),
            dma((2, 6, 2)),
            dma((6,)),
            dma((6,)),
            dma((6,)),
            dma((6,)),
            dma((2, pieces)),
            dma((2, pieces)),
            dma((2, pieces, groups - 1)),
            dma((2, pieces, groups - 1)),
            dma((2, pieces, groups)),
            dma((2, pieces, groups)),
            dma((2, 2, groups)),
            dma((2, 2, groups)),
            dma((2, 2, pieces, groups - 1)),
            dma((2, 2, pieces, groups - 1)),
            dma((2, pieces)),
            dma((2, pieces)),
        ],
        compiler_params=pltpu.CompilerParams(
            collective_id=0, has_side_effects=True, vmem_limit_bytes=60 * 2**20),
    )(flat(forward_state[0]), flat(returning_state[0]), flat(returning_grad[0]), weights[0],
      flat(fresh_input), flat(loss_grad))
    outs = pl.pallas_call(
        store,
        out_shape=tuple(jax.ShapeDtypeStruct(o.shape, o.dtype) for o in outs),
        in_specs=[pl.BlockSpec(memory_space=pl.ANY)] * 4,
        out_specs=(pl.BlockSpec(memory_space=pl.ANY),) * 4,
        scratch_shapes=[pltpu.VMEM(o.shape, o.dtype) for o in outs] + [dma((4,)), dma((4,))],
    )(*outs)
    shape = forward_state.shape
    return tuple(o.reshape(shape) for o in outs[:3]) + (outs[3][None],)


def solution(mesh):
    pair = P("segment", None, "band", None, None)
    whole = P(None, None, "band", None, None)
    return jax.shard_map(
        local,
        mesh=mesh,
        in_specs=(pair, pair, pair, P("segment", None, None, None), whole, whole),
        out_specs=(pair, pair, pair, P("segment", None, "band", None)),
        check_vma=False,
    )
```

```python
import functools

import jax
import jax.numpy as jnp
from jax import lax
from jax.experimental import pallas as pl
from jax.experimental.pallas import tpu as pltpu
from jax.sharding import PartitionSpec as P

MESH = pl.DeviceIdType.MESH
ACT_Q, ACT_OUT, ACT_Y, GRAD2, ACT_IN, BACK1 = range(6)
FWD1, FWD2, RET1, RET2, GRD1, GRD2 = range(6)
F, G = 0, 1
OWN, OTHER = 0, 1
TAKES = {ACT_Q: FWD2, ACT_Y: RET1, GRAD2: GRD2}
DEPTH = {FWD1: 1, FWD2: 2, RET1: 2, RET2: 1, GRD1: 1, GRD2: 2}


def kernel(segments, bands, width, pieces, fwd_in, ret_in, grd_in, weights_in, fresh_in, loss_in,
           fwd_out, ret_out, grd_out, wgrad_out,
           fields, wts, stack, sent, pulled, total, total_half, paired, reduced, partial, owned, ship_src, ship_dst,
           in_sem, w_sem, edge_sem, halo_send, halo_recv, mid_send, mid_recv, end_send, end_recv,
           wy_send, wy_recv, wx_send, wx_recv, wc_send, wc_recv,
           pair_send, pair_recv, red_send, red_recv, ship_send, ship_recv):
    seg = lax.axis_index("segment")
    band = lax.axis_index("band")
    pixels = sent.shape[2]
    channels = sent.shape[3]
    triple = 3 * channels
    chunk = partial.shape[3]
    margin = 2 * width
    inner = pl.ds(margin, pixels)
    first_pixels = pixels + 2 * width
    parity = lax.rem(seg, 2)
    even, odd = parity == 0, parity == 1
    other_seg = seg + 1 - 2 * parity
    first_seg, last_seg = seg == 0, seg == segments - 1
    below, above = seg >= 2, seg < segments - 2
    groups = bands // 2
    core, group = lax.rem(band, 2), band // 2
    core_band = band + 1 - 2 * core
    at_top, at_bottom = band == 0, band == bands - 1

    sources = {FWD1: fwd_in.at[0], FWD2: fwd_in.at[1], RET1: ret_in.at[0], RET2: ret_in.at[1],
               GRD1: grd_in.at[0], GRD2: grd_in.at[1]}

    def load(field):
        return pltpu.make_async_copy(sources[field], fields.at[0, field, inner], in_sem.at[field])

    def load_weights(index):
        return pltpu.make_async_copy(weights_in.at[index], wts.at[OWN, index], w_sem.at[index])

    load(RET1).start()
    load(GRD2).start()
    load_weights(G).start()
    load(RET2).start()
    load(GRD1).start()
    load_weights(F).start()
    load(FWD2).start()
    load(FWD1).start()

    barrier = pltpu.get_barrier_semaphore()
    for step in range(1, bands):
        pl.semaphore_signal(barrier, inc=1, device_id=(seg, lax.rem(band + step, bands)), device_id_type=MESH)
    pl.semaphore_signal(barrier, inc=1, device_id=(other_seg, band), device_id_type=MESH)

    @pl.when(below)
    def _():
        pl.semaphore_signal(barrier, inc=1, device_id=(seg - 2, band), device_id_type=MESH)

    @pl.when(above)
    def _():
        pl.semaphore_signal(barrier, inc=1, device_id=(seg + 2, band), device_id_type=MESH)

    def edge(which):
        return (
            pltpu.make_async_copy(fresh_in.at[0], fields.at[1, pl.ds(FWD1, 2), inner], edge_sem.at[0]),
            pltpu.make_async_copy(fresh_in.at[1], fwd_out, edge_sem.at[1]),
            pltpu.make_async_copy(loss_in.at[0], fields.at[1, pl.ds(GRD1, 2), inner], edge_sem.at[2]),
            pltpu.make_async_copy(loss_in.at[1], grd_out, edge_sem.at[3]),
        )[which]

    edge_places = (seg == 1, first_seg, seg == segments - 2, last_seg)
    for which in range(4):
        pl.when(edge_places[which])(edge(which).start)

    @pl.when(at_top)
    def _():
        fields[:, :, 0:margin] = jnp.zeros((2, 6, margin, channels), jnp.bfloat16)

    @pl.when(at_bottom)
    def _():
        fields[:, :, margin + pixels:] = jnp.zeros((2, 6, margin, channels), jnp.bfloat16)

    def halo_copy(tick, field, side):
        size = DEPTH[field] * width
        if side == 0:
            source, target = margin, margin + pixels
        else:
            source, target = margin + pixels - size, margin - size
        return pltpu.make_async_remote_copy(
            src_ref=fields.at[tick, field, pl.ds(source, size)], dst_ref=fields.at[tick, field, pl.ds(target, size)],
            send_sem=halo_send.at[tick, field, side], recv_sem=halo_recv.at[tick, field, 1 - side],
            device_id=(seg, band - 1 if side == 0 else band + 1), device_id_type=MESH)

    def send_halo(tick, field):
        pl.when(jnp.logical_not(at_top))(halo_copy(tick, field, 0).start)
        pl.when(jnp.logical_not(at_bottom))(halo_copy(tick, field, 1).start)

    def take_halo(tick, field):
        pl.when(jnp.logical_not(at_top))(halo_copy(tick, field, 1).wait_recv)
        pl.when(jnp.logical_not(at_bottom))(halo_copy(tick, field, 0).wait_recv)

    piece = chunk // pieces

    def w_rows(owner, part):
        return pl.ds(pl.multiple_of(owner * chunk + part * piece, piece), piece)

    def w_across(index, part):
        return pltpu.make_async_remote_copy(
            src_ref=wts.at[OWN, index, w_rows(band, part)], dst_ref=wts.at[OTHER, index, w_rows(band, part)],
            send_sem=wy_send.at[index, part], recv_sem=wy_recv.at[index, part],
            device_id=(other_seg, band), device_id_type=MESH)

    def w_group(index, part, step):
        rows = w_rows(band, part)
        return pltpu.make_async_remote_copy(
            src_ref=wts.at[OTHER, index, rows], dst_ref=wts.at[OTHER, index, rows],
            send_sem=wx_send.at[index, part, step - 1], recv_sem=wx_recv.at[index, part, step - 1],
            device_id=(seg, 2 * lax.rem(group + step, groups) + core), device_id_type=MESH)

    def w_core(index, part, step):
        rows = w_rows(2 * lax.rem(group + groups - step, groups) + core, part)
        return pltpu.make_async_remote_copy(
            src_ref=wts.at[OTHER, index, rows], dst_ref=wts.at[OTHER, index, rows],
            send_sem=wc_send.at[index, part, step], recv_sem=wc_recv.at[index, part, step],
            device_id=(seg, core_band), device_id_type=MESH)

    def w_direct(index, part, step):
        rows = w_rows(2 * lax.rem(group + groups - step, groups) + core, part)
        return pltpu.make_async_remote_copy(
            src_ref=wts.at[OWN, index, rows], dst_ref=wts.at[OTHER, index, rows],
            send_sem=wx_send.at[index, part, step - 1], recv_sem=wx_recv.at[index, part, step - 1],
            device_id=(other_seg, band), device_id_type=MESH)

    straight = jnp.logical_and(above, other_seg < segments - 2) if groups == 2 else jnp.bool_(False)

    def is_direct(index):
        return straight if index == F else jnp.bool_(False)

    def start_weights(index):
        for part in range(pieces):
            w_across(index, part).start()
            for step in range(1, groups):
                if index == F:
                    pl.when(is_direct(index))(w_direct(index, part, step).start)

    def spread_weights(index, part):
        w_across(index, part).wait_recv()
        for step in range(1, groups):
            pl.when(jnp.logical_not(is_direct(index)))(w_group(index, part, step).start)
        w_core(index, part, 0).start()

    def pass_weights(index, part):
        for step in range(1, groups):
            w_group(index, part, step).wait_recv()
            w_core(index, part, step).start()

    def take_weights(index):
        for part in range(pieces):
            for step in range(groups):
                w_core(index, part, step).wait_recv()

    def fill(slot, value, start=0):
        rows = value.shape[0]
        column = lax.rem(lax.broadcasted_iota(jnp.int32, (rows, channels), 0), width)
        wide = value.astype(jnp.float32)
        left = jnp.where(column == 0, 0.0, pltpu.roll(wide, 1, 0))
        right = jnp.where(column == width - 1, 0.0, pltpu.roll(wide, rows - 1, 0))
        stack[slot, start:start + rows, 0:channels] = left.astype(jnp.bfloat16)
        stack[slot, start:start + rows, channels:2 * channels] = value
        stack[slot, start:start + rows, 2 * channels:triple] = right.astype(jnp.bfloat16)

    def conv(slot, weight, rows):
        result = None
        for row in range(3):
            term = jnp.dot(stack[slot, row * width:row * width + rows], weight[row * triple:(row + 1) * triple],
                           preferred_element_type=jnp.float32)
            result = term if result is None else result + term
        return result

    def back(slot, weight, rows):
        result = None
        for tap in range(9):
            row, col = tap // 3, tap % 3
            start = (8 - tap) * channels
            term = lax.dot_general(stack[slot, row * width:row * width + rows, col * channels:(col + 1) * channels],
                                   weight[start:start + channels], (((1,), (1,)), ((), ())),
                                   preferred_element_type=jnp.float32)
            result = term if result is None else result + term
        return result

    def correlate(which, index, slot, offset, grads):
        for row in range(3):
            start = offset + row * width
            term = lax.dot_general(stack[slot, start:start + pixels], grads, (((0,), (0,)), ((), ())),
                                   preferred_element_type=jnp.float32)
            rows = slice(row * triple, (row + 1) * triple)
            total[which, index, rows] = term
            total_half[which, index, rows] = term.astype(jnp.bfloat16)

    def act(value):
        wide = value.astype(jnp.float32)
        return (wide * jax.nn.sigmoid(wide)).astype(jnp.bfloat16)

    def slope(value):
        wide = value.astype(jnp.float32)
        sigmoid = jax.nn.sigmoid(wide)
        return sigmoid * (1.0 + wide * (1.0 - sigmoid))

    place = lax.broadcasted_iota(jnp.int32, (first_pixels, channels), 0)
    inside = jnp.logical_and(place >= jnp.where(at_top, width, 0),
                             place < jnp.where(at_bottom, width + pixels, first_pixels))

    def trim(value):
        return jnp.where(inside, value, 0.0).astype(jnp.bfloat16)

    grown = slice(width, margin + pixels + width)
    core_rows = slice(margin, margin + pixels)
    kept = slice(width, width + pixels)

    class Tick:
        def __init__(self, tick, which, put, got):
            self.tick, self.which, self.put, self.got = tick, which, put, got

        def field(self, name, rows=core_rows):
            return fields[self.tick, name, rows]

        def weight(self, index):
            return wts.at[self.which, index]

        def advance_first(self):
            out1 = trim(self.field(FWD1, grown).astype(jnp.float32) + conv(ACT_Q, self.weight(F), first_pixels))
            self.put(FWD1, out1[kept])
            fill(ACT_OUT, act(out1))

        def advance_second(self):
            out2 = self.field(FWD2).astype(jnp.float32) + conv(ACT_OUT, self.weight(G), pixels)
            self.put(FWD2, out2.astype(jnp.bfloat16))

        def fill_inner(self, slot):
            value = self.field(TAKES[slot])
            fill(slot, value if slot == GRAD2 else act(value), margin)

        def fill_margins(self, slot):
            for start in (0, margin + pixels):
                value = fields[self.tick, TAKES[slot], start:start + margin]
                fill(slot, value if slot == GRAD2 else act(value), start)

        def invert_second(self):
            q2 = trim(self.field(RET2, grown).astype(jnp.float32) - conv(ACT_Y, self.weight(G), first_pixels))
            self.put(RET2, q2[kept])
            fill(ACT_IN, act(q2))

        def back_first(self):
            pulled[...] = slope(self.field(RET1, grown)) * back(GRAD2, self.weight(G), first_pixels)

        def back_inner(self):
            h1 = (self.field(GRD1).astype(jnp.float32) + pulled[kept]).astype(jnp.bfloat16)
            self.put(GRD1, h1)
            fill(BACK1, h1, width)

        def back_margins(self):
            for start, outside in ((0, at_top), (width + pixels, at_bottom)):
                rows = slice(start, start + width)
                grad = fields[self.tick, GRD1, start + width:start + 2 * width].astype(jnp.float32)
                fill(BACK1, jnp.where(outside, 0.0, grad + pulled[rows]).astype(jnp.bfloat16), start)

        def invert_first(self):
            p2 = self.field(RET1).astype(jnp.float32) - conv(ACT_IN, self.weight(F), pixels)
            self.put(RET1, p2.astype(jnp.bfloat16))

        def back_second(self):
            h2 = (self.field(GRD2).astype(jnp.float32)
                  + slope(self.got(RET2)) * back(BACK1, self.weight(F), pixels))
            self.put(GRD2, h2.astype(jnp.bfloat16))

        def correlate_g(self):
            correlate(self.tick, G, ACT_Y, width, self.field(GRD2))

        def correlate_f(self):
            correlate(self.tick, F, ACT_IN, 0, self.got(GRD1))

    def move(tick, field, target, device):
        return pltpu.make_async_remote_copy(
            src_ref=sent.at[tick, field], dst_ref=target[0], send_sem=(mid_send, end_send)[tick].at[field],
            recv_sem=(mid_recv, end_recv)[tick].at[target[1]], device_id=(device, band), device_id_type=MESH)

    def mid_target(field):
        return fields.at[1, field, inner], field

    def end_target(field):
        return (fwd_out, ret_out, grd_out)[field // 2].at[field % 2], field

    def mid_move(field):
        return move(0, field, mid_target(field), seg + 2 if field < RET1 else seg - 2)

    def turn_move(field):
        return move(0, field, mid_target(field + 2), seg - 1)

    def end_move(field):
        return move(1, field, end_target(field), seg + 2 if field < RET1 else seg - 2)

    def leave_move(field):
        return move(1, field, end_target(field + 2), seg + 1)

    mid_back = jnp.logical_and(even, below)
    mid_on = jnp.logical_and(odd, above)
    end_on = jnp.logical_and(even, above)
    end_back = jnp.logical_and(odd, below)
    leaves = seg == segments - 2

    def send_mid(field):
        if field < RET1:
            pl.when(mid_on)(mid_move(field).start)
            pl.when(last_seg)(turn_move(field).start)
        else:
            pl.when(mid_back)(mid_move(field).start)

    def put_mid(field, value):
        sent[0, field] = value
        if field != GRD1:
            send_mid(field)

        @pl.when(even if field < RET1 else odd)
        def _():
            fields[1, field, core_rows] = value

    def chunk_rows(owner):
        return pl.ds(pl.multiple_of(owner * chunk, chunk), chunk)

    def pair_copy(which, index, target):
        return pltpu.make_async_remote_copy(
            src_ref=total_half.at[which, index, chunk_rows(2 * target + 1 - core)],
            dst_ref=paired.at[which, index, target],
            send_sem=pair_send.at[which, index, target], recv_sem=pair_recv.at[which, index, target],
            device_id=(seg, core_band), device_id_type=MESH)

    def reduce_copy(which, index, part, step):
        rows = pl.ds(part * piece, piece)
        return pltpu.make_async_remote_copy(
            src_ref=reduced.at[which, index, step - 1, rows], dst_ref=partial.at[which, index, step - 1, rows],
            send_sem=red_send.at[which, index, part, step - 1], recv_sem=red_recv.at[which, index, part, step - 1],
            device_id=(seg, 2 * lax.rem(group + step, groups) + core), device_id_type=MESH)

    def ship_copy(index, part):
        rows = pl.ds(part * piece, piece)
        return pltpu.make_async_remote_copy(
            src_ref=ship_src.at[index, rows], dst_ref=ship_dst.at[index, rows],
            send_sem=ship_send.at[index, part], recv_sem=ship_recv.at[index, part],
            device_id=(other_seg, band), device_id_type=MESH)

    def start_sums(which, index):
        for target in range(groups):
            pair_copy(which, index, target).start()

    def pair_sum(which, index, target, part):
        rows = pl.ds(part * piece, piece)
        return (total[which, index, w_rows(2 * target + core, part)]
                + paired[which, index, target, rows].astype(jnp.float32))

    def pass_sums(which, index):
        for target in range(groups):
            pair_copy(which, index, target).wait_recv()
        for part in range(pieces):
            rows = pl.ds(part * piece, piece)
            for step in range(1, groups):
                value = pair_sum(which, index, lax.rem(group + step, groups), part)
                reduced[which, index, step - 1, rows] = value.astype(jnp.bfloat16)
                reduce_copy(which, index, part, step).start()

    def finish_sums(which, index, part):
        value = pair_sum(which, index, group, part)
        for step in range(1, groups):
            reduce_copy(which, index, part, step).wait_recv()
            value = value + partial[which, index, step - 1, pl.ds(part * piece, piece)].astype(jnp.float32)
        return value

    def keep_sums(index):
        for part in range(pieces):
            owned[index, pl.ds(part * piece, piece)] = finish_sums(OWN, index, part)

    def ship_sums(index):
        for part in range(pieces):
            ship_src[index, pl.ds(part * piece, piece)] = finish_sums(OTHER, index, part).astype(jnp.bfloat16)
            ship_copy(index, part).start()

    def close_sums(index):
        for part in range(pieces):
            rows = pl.ds(part * piece, piece)
            ship_copy(index, part).wait_recv()
            wgrad_out[index, rows] = owned[index, rows] + ship_dst[index, rows].astype(jnp.float32)

    first = Tick(0, OWN, put_mid, lambda field: sent[0, field])
    load(RET1).wait()
    first.fill_inner(ACT_Y)
    load(GRD2).wait()
    first.fill_inner(GRAD2)
    load(FWD2).wait()
    first.fill_inner(ACT_Q)
    load(RET2).wait()
    load(GRD1).wait()
    load(FWD1).wait()
    load_weights(G).wait()
    load_weights(F).wait()
    neighbours = below.astype(jnp.int32) + above.astype(jnp.int32)
    pl.semaphore_wait(barrier, bands + neighbours)
    for field in (RET1, RET2, GRD2, GRD1, FWD2, FWD1):
        send_halo(0, field)
    start_weights(G)
    start_weights(F)

    take_halo(0, RET1)
    first.fill_margins(ACT_Y)
    take_halo(0, RET2)
    first.invert_second()
    take_halo(0, GRD2)
    first.fill_margins(GRAD2)
    first.back_first()
    take_halo(0, GRD1)
    first.back_inner()
    first.back_margins()
    spread_weights(G, 0)
    first.invert_first()
    first.back_second()
    send_mid(GRD1)

    @pl.when(odd)
    def _():
        for field in (RET1, RET2, GRD2, GRD1):
            send_halo(1, field)

    first.correlate_g()
    start_sums(OWN, G)
    for part in range(1, pieces):
        spread_weights(G, part)
    first.correlate_f()
    start_sums(OWN, F)
    shared = jnp.logical_not(straight)

    @pl.when(shared)
    def _():
        spread_weights(F, 0)

    take_halo(0, FWD2)
    first.fill_margins(ACT_Q)
    take_halo(0, FWD1)
    first.advance_first()

    @pl.when(shared)
    def _():
        for part in range(1, pieces):
            spread_weights(F, part)

    @pl.when(straight)
    def _():
        pass_sums(OWN, G)

    for part in range(pieces):
        pass_weights(G, part)
    first.advance_second()

    @pl.when(even)
    def _():
        for field in (FWD2, FWD1):
            send_halo(1, field)

    @pl.when(shared)
    def _():
        pass_sums(OWN, G)

    @pl.when(odd)
    def _():
        def put(field, value):
            if field < RET1:
                fwd_out[field] = value
            else:
                sent[1, field] = value
                pl.when(end_back)(end_move(field).start)

        last = Tick(1, OTHER, put, lambda field: sent[1, field])
        last.fill_inner(ACT_Y)
        last.fill_inner(GRAD2)
        take_halo(1, RET1)
        last.fill_margins(ACT_Y)
        take_halo(1, GRD2)
        last.fill_margins(GRAD2)
        last.correlate_g()
        start_sums(OTHER, G)
        take_halo(1, RET2)
        take_halo(1, GRD1)
        take_weights(G)
        last.invert_second()
        last.back_first()
        last.back_inner()
        last.back_margins()
        pass_sums(OTHER, G)
        last.correlate_f()
        start_sums(OTHER, F)

        @pl.when(straight)
        def _():
            for part in range(pieces):
                spread_weights(F, part)

        for field in (FWD2, FWD1):
            pl.when(below)(mid_move(field).wait_recv)
        pl.when(seg == 1)(edge(0).wait)
        for field in (FWD2, FWD1):
            send_halo(1, field)
        for part in range(pieces):
            pass_weights(F, part)
        pass_sums(OTHER, F)
        pass_sums(OWN, F)

        take_weights(F)
        last.invert_first()
        last.back_second()
        last.fill_inner(ACT_Q)
        ship_sums(G)
        for field in (FWD2, FWD1):
            take_halo(1, field)
        last.fill_margins(ACT_Q)
        last.advance_first()
        last.advance_second()
        keep_sums(G)
        ship_sums(F)
        keep_sums(F)

    @pl.when(even)
    def _():
        def put(field, value):
            if field < RET1:
                sent[1, field] = value
                pl.when(end_on)(end_move(field).start)
                pl.when(leaves)(leave_move(field).start)
            else:
                (ret_out, grd_out)[field // 2 - 1][field % 2] = value

        last = Tick(1, OTHER, put, lambda field: (ret_out, grd_out)[field // 2 - 1][field % 2])

        def arrive(field):
            if field < GRD1:
                mid_move(field).wait_recv()
            else:
                pl.when(above)(mid_move(field).wait_recv)
                if field == GRD2:
                    pl.when(leaves)(edge(2).wait)
            send_halo(1, field)

        @pl.when(straight)
        def _():
            arrive(RET2)
            arrive(RET1)
            last.fill_inner(ACT_Y)
            last.fill_inner(ACT_Q)
            for field in (FWD2, FWD1):
                take_halo(1, field)
            last.fill_margins(ACT_Q)
            take_halo(1, RET1)
            last.fill_margins(ACT_Y)
            take_weights(G)
            take_halo(1, RET2)
            last.invert_second()
            for part in range(pieces):
                spread_weights(F, part)
            arrive(GRD2)
            last.correlate_g()
            start_sums(OTHER, G)
            for part in range(pieces):
                pass_weights(F, part)
            take_weights(F)
            last.advance_first()
            last.fill_inner(GRAD2)
            take_halo(1, GRD2)
            last.fill_margins(GRAD2)
            pass_sums(OTHER, G)
            last.back_first()
            arrive(GRD1)
            last.back_inner()
            last.correlate_f()
            start_sums(OTHER, F)
            last.advance_second()

        @pl.when(shared)
        def _():
            arrive(GRD2)
            arrive(GRD1)
            last.fill_inner(GRAD2)
            last.fill_inner(ACT_Q)
            for part in range(pieces):
                pass_weights(F, part)
            for field in (FWD2, FWD1):
                take_halo(1, field)
            last.fill_margins(ACT_Q)
            take_weights(G)
            take_weights(F)
            last.advance_first()
            last.advance_second()
            arrive(RET1)
            last.fill_inner(ACT_Y)
            take_halo(1, RET1)
            last.fill_margins(ACT_Y)
            last.correlate_g()
            start_sums(OTHER, G)
            take_halo(1, GRD2)
            last.fill_margins(GRAD2)
            last.back_first()
            last.back_inner()
            arrive(RET2)
            pass_sums(OTHER, G)
            take_halo(1, RET2)
            last.invert_second()
            last.correlate_f()
            start_sums(OTHER, F)
            last.invert_first()

        pass_sums(OTHER, F)
        pass_sums(OWN, F)

        @pl.when(straight)
        def _():
            last.invert_first()

        take_halo(1, GRD1)
        last.back_margins()
        last.back_second()
        keep_sums(G)
        ship_sums(G)
        ship_sums(F)
        keep_sums(F)

    pl.when(first_seg)(edge(1).wait)
    pl.when(last_seg)(edge(3).wait)
    for field in (FWD1, FWD2):
        pl.when(jnp.logical_and(even, below))(end_move(field).wait_recv)
        pl.when(last_seg)(end_move(field + 2).wait_recv)
    for field in (RET1, RET2, GRD1, GRD2):
        pl.when(jnp.logical_and(odd, above))(end_move(field).wait_recv)

    for field in range(6):
        for tick in range(2):
            pl.when(jnp.logical_not(at_top))(halo_copy(tick, field, 0).wait_send)
            pl.when(jnp.logical_not(at_bottom))(halo_copy(tick, field, 1).wait_send)
        if field < RET1:
            pl.when(mid_on)(mid_move(field).wait_send)
            pl.when(last_seg)(turn_move(field).wait_send)
            pl.when(end_on)(end_move(field).wait_send)
            pl.when(leaves)(leave_move(field).wait_send)
        else:
            pl.when(mid_back)(mid_move(field).wait_send)
            pl.when(end_back)(end_move(field).wait_send)
    for index in range(2):
        for part in range(pieces):
            w_across(index, part).wait_send()
            for step in range(1, groups):
                w_group(index, part, step).wait_send()
            for step in range(groups):
                w_core(index, part, step).wait_send()
        for which in range(2):
            for target in range(groups):
                pair_copy(which, index, target).wait_send()
            for part in range(pieces):
                for step in range(1, groups):
                    reduce_copy(which, index, part, step).wait_send()

    close_sums(G)
    close_sums(F)
    for index in range(2):
        for part in range(pieces):
            ship_copy(index, part).wait_send()


def store(*refs):
    count = (len(refs) - 2) // 3
    sources, targets, held = refs[:count], refs[count:2 * count], refs[2 * count:3 * count]
    load_sem, store_sem = refs[3 * count:]
    loads = [pltpu.make_async_copy(sources[i], held[i], load_sem.at[i]) for i in range(count)]
    stores = [pltpu.make_async_copy(held[i], targets[i], store_sem.at[i]) for i in range(count)]
    for load in loads:
        load.start()
    for load, out in zip(loads, stores):
        load.wait()
        out.start()
    for out in stores:
        out.wait()


def local(forward_state, returning_state, returning_grad, weights, fresh_input, loss_grad):
    segments, bands = lax.axis_size("segment"), lax.axis_size("band")
    _, _, rows, width, channels = forward_state.shape
    pixels = rows * width
    taps = weights.shape[2]
    chunk = taps // bands
    groups = bands // 2
    pieces = next(count for count in (2, 1) if chunk % (16 * count) == 0 or count == 1)
    assert fresh_input.shape[0] == 2 and segments % 2 == 0 and bands % 2 == 0 and rows >= 2
    bf16, f32 = jnp.bfloat16, jnp.float32
    pair = jax.ShapeDtypeStruct((2, pixels, channels), bf16)
    dma = pltpu.SemaphoreType.DMA
    flat = lambda x: x.reshape(x.shape[:-3] + (pixels, channels))
    vmem = pl.BlockSpec(memory_space=pltpu.VMEM)
    outs = pl.pallas_call(
        functools.partial(kernel, segments, bands, width, pieces),
        out_shape=(pair, pair, pair, jax.ShapeDtypeStruct((2, chunk, channels), f32)),
        in_specs=[pl.BlockSpec(memory_space=pl.ANY)] * 6,
        out_specs=(vmem,) * 4,
        scratch_shapes=[
            pltpu.VMEM((2, 6, pixels + 4 * width, channels), bf16),
            pltpu.VMEM((2, 2, taps, channels), bf16),
            pltpu.VMEM((6, pixels + 4 * width, 3 * channels), bf16),
            pltpu.VMEM((2, 6, pixels, channels), bf16),
            pltpu.VMEM((pixels + 2 * width, channels), f32),
            pltpu.VMEM((2, 2, taps, channels), f32),
            pltpu.VMEM((2, 2, taps, channels), bf16),
            pltpu.VMEM((2, 2, groups, chunk, channels), bf16),
            pltpu.VMEM((2, 2, groups - 1, chunk, channels), bf16),
            pltpu.VMEM((2, 2, groups - 1, chunk, channels), bf16),
            pltpu.VMEM((2, chunk, channels), f32),
            pltpu.VMEM((2, chunk, channels), bf16),
            pltpu.VMEM((2, chunk, channels), bf16),
            dma((6,)),
            dma((2,)),
            dma((4,)),
            dma((2, 6, 2)),
            dma((2, 6, 2)),
            dma((6,)),
            dma((6,)),
            dma((6,)),
            dma((6,)),
            dma((2, pieces)),
            dma((2, pieces)),
            dma((2, pieces, groups - 1)),
            dma((2, pieces, groups - 1)),
            dma((2, pieces, groups)),
            dma((2, pieces, groups)),
            dma((2, 2, groups)),
            dma((2, 2, groups)),
            dma((2, 2, pieces, groups - 1)),
            dma((2, 2, pieces, groups - 1)),
            dma((2, pieces)),
            dma((2, pieces)),
        ],
        compiler_params=pltpu.CompilerParams(
            collective_id=0, has_side_effects=True, vmem_limit_bytes=60 * 2**20),
    )(flat(forward_state[0]), flat(returning_state[0]), flat(returning_grad[0]), weights[0],
      flat(fresh_input), flat(loss_grad))
    outs = pl.pallas_call(
        store,
        out_shape=tuple(jax.ShapeDtypeStruct(o.shape, o.dtype) for o in outs),
        in_specs=[pl.BlockSpec(memory_space=pl.ANY)] * 4,
        out_specs=(pl.BlockSpec(memory_space=pl.ANY),) * 4,
        scratch_shapes=[pltpu.VMEM(o.shape, o.dtype) for o in outs] + [dma((4,)), dma((4,))],
    )(*outs)
    shape = forward_state.shape
    return tuple(o.reshape(shape) for o in outs[:3]) + (outs[3][None],)


def solution(mesh):
    pair = P("segment", None, "band", None, None)
    whole = P(None, None, "band", None, None)
    return jax.shard_map(
        local,
        mesh=mesh,
        in_specs=(pair, pair, pair, P("segment", None, None, None), whole, whole),
        out_specs=(pair, pair, pair, P("segment", None, "band", None)),
        check_vma=False,
    )
```

```python
import functools

import jax
import jax.numpy as jnp
from jax import lax
from jax.experimental import pallas as pl
from jax.experimental.pallas import tpu as pltpu
from jax.sharding import PartitionSpec as P

MESH = pl.DeviceIdType.MESH
ACT_Q, ACT_OUT, ACT_Y, GRAD2, ACT_IN, BACK1 = range(6)
FWD1, FWD2, RET1, RET2, GRD1, GRD2 = range(6)
F, G = 0, 1
OWN, OTHER = 0, 1
TAKES = {ACT_Q: FWD2, ACT_Y: RET1, GRAD2: GRD2}
DEPTH = {FWD1: 1, FWD2: 2, RET1: 2, RET2: 1, GRD1: 1, GRD2: 2}


def kernel(segments, bands, width, pieces, fwd_in, ret_in, grd_in, weights_in, fresh_in, loss_in,
           fwd_out, ret_out, grd_out, wgrad_out,
           fields, wts, stack, sent, pulled, total, total_half, paired, reduced, partial, owned, ship_src, ship_dst,
           in_sem, w_sem, edge_sem, halo_send, halo_recv, mid_send, mid_recv, end_send, end_recv,
           wy_send, wy_recv, wx_send, wx_recv, wc_send, wc_recv,
           pair_send, pair_recv, red_send, red_recv, ship_send, ship_recv):
    seg = lax.axis_index("segment")
    band = lax.axis_index("band")
    pixels = sent.shape[2]
    channels = sent.shape[3]
    triple = 3 * channels
    chunk = partial.shape[3]
    margin = 2 * width
    inner = pl.ds(margin, pixels)
    first_pixels = pixels + 2 * width
    parity = lax.rem(seg, 2)
    even, odd = parity == 0, parity == 1
    other_seg = seg + 1 - 2 * parity
    first_seg, last_seg = seg == 0, seg == segments - 1
    below, above = seg >= 2, seg < segments - 2
    groups = bands // 2
    core, group = lax.rem(band, 2), band // 2
    core_band = band + 1 - 2 * core
    at_top, at_bottom = band == 0, band == bands - 1

    sources = {FWD1: fwd_in.at[0], FWD2: fwd_in.at[1], RET1: ret_in.at[0], RET2: ret_in.at[1],
               GRD1: grd_in.at[0], GRD2: grd_in.at[1]}

    def load(field):
        return pltpu.make_async_copy(sources[field], fields.at[0, field, inner], in_sem.at[field])

    def load_weights(index):
        return pltpu.make_async_copy(weights_in.at[index], wts.at[OWN, index], w_sem.at[index])

    load(RET1).start()
    load(GRD2).start()
    load_weights(G).start()
    load(RET2).start()
    load(GRD1).start()
    load_weights(F).start()
    load(FWD2).start()
    load(FWD1).start()

    barrier = pltpu.get_barrier_semaphore()
    for step in range(1, bands):
        pl.semaphore_signal(barrier, inc=1, device_id=(seg, lax.rem(band + step, bands)), device_id_type=MESH)
    pl.semaphore_signal(barrier, inc=1, device_id=(other_seg, band), device_id_type=MESH)

    @pl.when(below)
    def _():
        pl.semaphore_signal(barrier, inc=1, device_id=(seg - 2, band), device_id_type=MESH)

    @pl.when(above)
    def _():
        pl.semaphore_signal(barrier, inc=1, device_id=(seg + 2, band), device_id_type=MESH)

    def edge(which):
        return (
            pltpu.make_async_copy(fresh_in.at[0], fields.at[1, pl.ds(FWD1, 2), inner], edge_sem.at[0]),
            pltpu.make_async_copy(fresh_in.at[1], fwd_out, edge_sem.at[1]),
            pltpu.make_async_copy(loss_in.at[0], fields.at[1, pl.ds(GRD1, 2), inner], edge_sem.at[2]),
            pltpu.make_async_copy(loss_in.at[1], grd_out, edge_sem.at[3]),
        )[which]

    edge_places = (seg == 1, first_seg, seg == segments - 2, last_seg)
    for which in range(4):
        pl.when(edge_places[which])(edge(which).start)

    @pl.when(at_top)
    def _():
        fields[:, :, 0:margin] = jnp.zeros((2, 6, margin, channels), jnp.bfloat16)

    @pl.when(at_bottom)
    def _():
        fields[:, :, margin + pixels:] = jnp.zeros((2, 6, margin, channels), jnp.bfloat16)

    def halo_copy(tick, field, side):
        size = DEPTH[field] * width
        if side == 0:
            source, target = margin, margin + pixels
        else:
            source, target = margin + pixels - size, margin - size
        return pltpu.make_async_remote_copy(
            src_ref=fields.at[tick, field, pl.ds(source, size)], dst_ref=fields.at[tick, field, pl.ds(target, size)],
            send_sem=halo_send.at[tick, field, side], recv_sem=halo_recv.at[tick, field, 1 - side],
            device_id=(seg, band - 1 if side == 0 else band + 1), device_id_type=MESH)

    def send_halo(tick, field):
        pl.when(jnp.logical_not(at_top))(halo_copy(tick, field, 0).start)
        pl.when(jnp.logical_not(at_bottom))(halo_copy(tick, field, 1).start)

    def take_halo(tick, field):
        pl.when(jnp.logical_not(at_top))(halo_copy(tick, field, 1).wait_recv)
        pl.when(jnp.logical_not(at_bottom))(halo_copy(tick, field, 0).wait_recv)

    piece = chunk // pieces

    def w_rows(owner, part):
        return pl.ds(pl.multiple_of(owner * chunk + part * piece, piece), piece)

    def w_across(index, part):
        return pltpu.make_async_remote_copy(
            src_ref=wts.at[OWN, index, w_rows(band, part)], dst_ref=wts.at[OTHER, index, w_rows(band, part)],
            send_sem=wy_send.at[index, part], recv_sem=wy_recv.at[index, part],
            device_id=(other_seg, band), device_id_type=MESH)

    def w_group(index, part, step):
        rows = w_rows(band, part)
        return pltpu.make_async_remote_copy(
            src_ref=wts.at[OTHER, index, rows], dst_ref=wts.at[OTHER, index, rows],
            send_sem=wx_send.at[index, part, step - 1], recv_sem=wx_recv.at[index, part, step - 1],
            device_id=(seg, 2 * lax.rem(group + step, groups) + core), device_id_type=MESH)

    def w_core(index, part, step):
        rows = w_rows(2 * lax.rem(group + groups - step, groups) + core, part)
        return pltpu.make_async_remote_copy(
            src_ref=wts.at[OTHER, index, rows], dst_ref=wts.at[OTHER, index, rows],
            send_sem=wc_send.at[index, part, step], recv_sem=wc_recv.at[index, part, step],
            device_id=(seg, core_band), device_id_type=MESH)

    def w_direct(index, part, step):
        rows = w_rows(2 * lax.rem(group + groups - step, groups) + core, part)
        return pltpu.make_async_remote_copy(
            src_ref=wts.at[OWN, index, rows], dst_ref=wts.at[OTHER, index, rows],
            send_sem=wx_send.at[index, part, step - 1], recv_sem=wx_recv.at[index, part, step - 1],
            device_id=(other_seg, band), device_id_type=MESH)

    straight = jnp.logical_and(above, other_seg < segments - 2) if groups == 2 else jnp.bool_(False)

    def is_direct(index):
        return straight if index == F else jnp.bool_(False)

    def start_weights(index):
        for part in range(pieces):
            w_across(index, part).start()
            for step in range(1, groups):
                if index == F:
                    pl.when(is_direct(index))(w_direct(index, part, step).start)

    def spread_weights(index, part):
        w_across(index, part).wait_recv()
        for step in range(1, groups):
            pl.when(jnp.logical_not(is_direct(index)))(w_group(index, part, step).start)
        w_core(index, part, 0).start()

    def pass_weights(index, part):
        for step in range(1, groups):
            w_group(index, part, step).wait_recv()
            w_core(index, part, step).start()

    def take_weights(index):
        for part in range(pieces):
            for step in range(groups):
                w_core(index, part, step).wait_recv()

    def fill(slot, value, start=0):
        rows = value.shape[0]
        column = lax.rem(lax.broadcasted_iota(jnp.int32, (rows, channels), 0), width)
        wide = value.astype(jnp.float32)
        left = jnp.where(column == 0, 0.0, pltpu.roll(wide, 1, 0))
        right = jnp.where(column == width - 1, 0.0, pltpu.roll(wide, rows - 1, 0))
        stack[slot, start:start + rows, 0:channels] = left.astype(jnp.bfloat16)
        stack[slot, start:start + rows, channels:2 * channels] = value
        stack[slot, start:start + rows, 2 * channels:triple] = right.astype(jnp.bfloat16)

    def conv(slot, weight, rows):
        result = None
        for row in range(3):
            term = jnp.dot(stack[slot, row * width:row * width + rows], weight[row * triple:(row + 1) * triple],
                           preferred_element_type=jnp.float32)
            result = term if result is None else result + term
        return result

    def back(slot, weight, rows):
        result = None
        for tap in range(9):
            row, col = tap // 3, tap % 3
            start = (8 - tap) * channels
            term = lax.dot_general(stack[slot, row * width:row * width + rows, col * channels:(col + 1) * channels],
                                   weight[start:start + channels], (((1,), (1,)), ((), ())),
                                   preferred_element_type=jnp.float32)
            result = term if result is None else result + term
        return result

    def correlate(which, index, slot, offset, grads):
        for row in range(3):
            start = offset + row * width
            term = lax.dot_general(stack[slot, start:start + pixels], grads, (((0,), (0,)), ((), ())),
                                   preferred_element_type=jnp.float32)
            rows = slice(row * triple, (row + 1) * triple)
            total[which, index, rows] = term
            total_half[which, index, rows] = term.astype(jnp.bfloat16)

    def act(value):
        wide = value.astype(jnp.float32)
        return (wide * jax.nn.sigmoid(wide)).astype(jnp.bfloat16)

    def slope(value):
        wide = value.astype(jnp.float32)
        sigmoid = jax.nn.sigmoid(wide)
        return sigmoid * (1.0 + wide * (1.0 - sigmoid))

    place = lax.broadcasted_iota(jnp.int32, (first_pixels, channels), 0)
    inside = jnp.logical_and(place >= jnp.where(at_top, width, 0),
                             place < jnp.where(at_bottom, width + pixels, first_pixels))

    def trim(value):
        return jnp.where(inside, value, 0.0).astype(jnp.bfloat16)

    grown = slice(width, margin + pixels + width)
    core_rows = slice(margin, margin + pixels)
    kept = slice(width, width + pixels)

    class Tick:
        def __init__(self, tick, which, put, got):
            self.tick, self.which, self.put, self.got = tick, which, put, got

        def field(self, name, rows=core_rows):
            return fields[self.tick, name, rows]

        def weight(self, index):
            return wts.at[self.which, index]

        def advance_first(self):
            out1 = trim(self.field(FWD1, grown).astype(jnp.float32) + conv(ACT_Q, self.weight(F), first_pixels))
            self.put(FWD1, out1[kept])
            fill(ACT_OUT, act(out1))

        def advance_second(self):
            out2 = self.field(FWD2).astype(jnp.float32) + conv(ACT_OUT, self.weight(G), pixels)
            self.put(FWD2, out2.astype(jnp.bfloat16))

        def fill_inner(self, slot):
            value = self.field(TAKES[slot])
            fill(slot, value if slot == GRAD2 else act(value), margin)

        def fill_margins(self, slot):
            for start in (0, margin + pixels):
                value = fields[self.tick, TAKES[slot], start:start + margin]
                fill(slot, value if slot == GRAD2 else act(value), start)

        def invert_second(self):
            q2 = trim(self.field(RET2, grown).astype(jnp.float32) - conv(ACT_Y, self.weight(G), first_pixels))
            self.put(RET2, q2[kept])
            fill(ACT_IN, act(q2))

        def back_first(self):
            pulled[...] = slope(self.field(RET1, grown)) * back(GRAD2, self.weight(G), first_pixels)

        def back_inner(self):
            h1 = (self.field(GRD1).astype(jnp.float32) + pulled[kept]).astype(jnp.bfloat16)
            self.put(GRD1, h1)
            fill(BACK1, h1, width)

        def back_margins(self):
            for start, outside in ((0, at_top), (width + pixels, at_bottom)):
                rows = slice(start, start + width)
                grad = fields[self.tick, GRD1, start + width:start + 2 * width].astype(jnp.float32)
                fill(BACK1, jnp.where(outside, 0.0, grad + pulled[rows]).astype(jnp.bfloat16), start)

        def invert_first(self):
            p2 = self.field(RET1).astype(jnp.float32) - conv(ACT_IN, self.weight(F), pixels)
            self.put(RET1, p2.astype(jnp.bfloat16))

        def back_second(self):
            h2 = (self.field(GRD2).astype(jnp.float32)
                  + slope(self.got(RET2)) * back(BACK1, self.weight(F), pixels))
            self.put(GRD2, h2.astype(jnp.bfloat16))

        def correlate_g(self):
            correlate(self.tick, G, ACT_Y, width, self.field(GRD2))

        def correlate_f(self):
            correlate(self.tick, F, ACT_IN, 0, self.got(GRD1))

    def move(tick, field, target, device):
        return pltpu.make_async_remote_copy(
            src_ref=sent.at[tick, field], dst_ref=target[0], send_sem=(mid_send, end_send)[tick].at[field],
            recv_sem=(mid_recv, end_recv)[tick].at[target[1]], device_id=(device, band), device_id_type=MESH)

    def mid_target(field):
        return fields.at[1, field, inner], field

    def end_target(field):
        return (fwd_out, ret_out, grd_out)[field // 2].at[field % 2], field

    def mid_move(field):
        return move(0, field, mid_target(field), seg + 2 if field < RET1 else seg - 2)

    def turn_move(field):
        return move(0, field, mid_target(field + 2), seg - 1)

    def end_move(field):
        return move(1, field, end_target(field), seg + 2 if field < RET1 else seg - 2)

    def leave_move(field):
        return move(1, field, end_target(field + 2), seg + 1)

    mid_back = jnp.logical_and(even, below)
    mid_on = jnp.logical_and(odd, above)
    end_on = jnp.logical_and(even, above)
    end_back = jnp.logical_and(odd, below)
    leaves = seg == segments - 2

    def send_mid(field):
        if field < RET1:
            pl.when(mid_on)(mid_move(field).start)
            pl.when(last_seg)(turn_move(field).start)
        else:
            pl.when(mid_back)(mid_move(field).start)

    def put_mid(field, value):
        sent[0, field] = value
        if field != GRD1:
            send_mid(field)

        @pl.when(even if field < RET1 else odd)
        def _():
            fields[1, field, core_rows] = value

    def chunk_rows(owner):
        return pl.ds(pl.multiple_of(owner * chunk, chunk), chunk)

    def pair_copy(which, index, target):
        return pltpu.make_async_remote_copy(
            src_ref=total_half.at[which, index, chunk_rows(2 * target + 1 - core)],
            dst_ref=paired.at[which, index, target],
            send_sem=pair_send.at[which, index, target], recv_sem=pair_recv.at[which, index, target],
            device_id=(seg, core_band), device_id_type=MESH)

    def reduce_copy(which, index, part, step):
        rows = pl.ds(part * piece, piece)
        return pltpu.make_async_remote_copy(
            src_ref=reduced.at[which, index, step - 1, rows], dst_ref=partial.at[which, index, step - 1, rows],
            send_sem=red_send.at[which, index, part, step - 1], recv_sem=red_recv.at[which, index, part, step - 1],
            device_id=(seg, 2 * lax.rem(group + step, groups) + core), device_id_type=MESH)

    def ship_copy(index, part):
        rows = pl.ds(part * piece, piece)
        return pltpu.make_async_remote_copy(
            src_ref=ship_src.at[index, rows], dst_ref=ship_dst.at[index, rows],
            send_sem=ship_send.at[index, part], recv_sem=ship_recv.at[index, part],
            device_id=(other_seg, band), device_id_type=MESH)

    def start_sums(which, index):
        for target in range(groups):
            pair_copy(which, index, target).start()

    def pair_sum(which, index, target, part):
        rows = pl.ds(part * piece, piece)
        return (total[which, index, w_rows(2 * target + core, part)]
                + paired[which, index, target, rows].astype(jnp.float32))

    early, late = range((pieces + 1) // 2), range((pieces + 1) // 2, pieces)

    def pass_sums(which, index, parts=range(pieces)):
        if 0 in parts:
            for target in range(groups):
                pair_copy(which, index, target).wait_recv()
        for part in parts:
            rows = pl.ds(part * piece, piece)
            for step in range(1, groups):
                value = pair_sum(which, index, lax.rem(group + step, groups), part)
                reduced[which, index, step - 1, rows] = value.astype(jnp.bfloat16)
                reduce_copy(which, index, part, step).start()

    def finish_sums(which, index, part):
        value = pair_sum(which, index, group, part)
        for step in range(1, groups):
            reduce_copy(which, index, part, step).wait_recv()
            value = value + partial[which, index, step - 1, pl.ds(part * piece, piece)].astype(jnp.float32)
        return value

    def keep_sums(index):
        for part in range(pieces):
            owned[index, pl.ds(part * piece, piece)] = finish_sums(OWN, index, part)

    def ship_sums(index):
        for part in range(pieces):
            ship_src[index, pl.ds(part * piece, piece)] = finish_sums(OTHER, index, part).astype(jnp.bfloat16)
            ship_copy(index, part).start()

    def close_sums(index):
        for part in range(pieces):
            rows = pl.ds(part * piece, piece)
            ship_copy(index, part).wait_recv()
            wgrad_out[index, rows] = owned[index, rows] + ship_dst[index, rows].astype(jnp.float32)

    first = Tick(0, OWN, put_mid, lambda field: sent[0, field])
    load(RET1).wait()
    first.fill_inner(ACT_Y)
    load(GRD2).wait()
    first.fill_inner(GRAD2)
    load(FWD2).wait()
    first.fill_inner(ACT_Q)
    load(RET2).wait()
    load(GRD1).wait()
    load(FWD1).wait()
    load_weights(G).wait()
    load_weights(F).wait()
    neighbours = below.astype(jnp.int32) + above.astype(jnp.int32)
    pl.semaphore_wait(barrier, bands + neighbours)
    for field in (RET1, RET2, GRD2, GRD1, FWD2, FWD1):
        send_halo(0, field)
    start_weights(G)
    start_weights(F)

    take_halo(0, RET1)
    first.fill_margins(ACT_Y)
    take_halo(0, RET2)
    first.invert_second()
    take_halo(0, GRD2)
    first.fill_margins(GRAD2)
    first.back_first()
    take_halo(0, GRD1)
    first.back_inner()
    first.back_margins()
    spread_weights(G, 0)
    first.invert_first()
    first.back_second()
    send_mid(GRD1)

    @pl.when(odd)
    def _():
        for field in (RET1, RET2, GRD2, GRD1):
            send_halo(1, field)

    first.correlate_g()
    start_sums(OWN, G)
    for part in range(1, pieces):
        spread_weights(G, part)
    first.correlate_f()
    start_sums(OWN, F)
    shared = jnp.logical_not(straight)

    @pl.when(jnp.logical_and(straight, even))
    def _():
        pass_sums(OWN, G, early)

    @pl.when(shared)
    def _():
        spread_weights(F, 0)

    take_halo(0, FWD2)
    first.fill_margins(ACT_Q)
    take_halo(0, FWD1)
    first.advance_first()

    @pl.when(shared)
    def _():
        for part in range(1, pieces):
            spread_weights(F, part)

    @pl.when(jnp.logical_and(straight, odd))
    def _():
        pass_sums(OWN, G)
        pass_sums(OWN, F)

    for part in range(pieces):
        pass_weights(G, part)
    first.advance_second()

    @pl.when(even)
    def _():
        for field in (FWD2, FWD1):
            send_halo(1, field)

    @pl.when(shared)
    def _():
        pass_sums(OWN, G)

    @pl.when(odd)
    def _():
        def put(field, value):
            if field < RET1:
                fwd_out[field] = value
            else:
                sent[1, field] = value
                pl.when(end_back)(end_move(field).start)

        last = Tick(1, OTHER, put, lambda field: sent[1, field])
        last.fill_inner(ACT_Y)
        last.fill_inner(GRAD2)
        take_halo(1, RET1)
        last.fill_margins(ACT_Y)
        take_halo(1, GRD2)
        last.fill_margins(GRAD2)
        last.correlate_g()
        start_sums(OTHER, G)
        take_halo(1, RET2)
        take_halo(1, GRD1)
        take_weights(G)
        last.invert_second()
        last.back_first()
        last.back_inner()
        last.back_margins()
        pass_sums(OTHER, G)
        last.correlate_f()
        start_sums(OTHER, F)

        @pl.when(straight)
        def _():
            for part in range(pieces):
                spread_weights(F, part)

        for field in (FWD2, FWD1):
            pl.when(below)(mid_move(field).wait_recv)
        pl.when(seg == 1)(edge(0).wait)
        for field in (FWD2, FWD1):
            send_halo(1, field)
        for part in range(pieces):
            pass_weights(F, part)
        pass_sums(OTHER, F)

        @pl.when(shared)
        def _():
            pass_sums(OWN, F)


        take_weights(F)
        last.invert_first()
        last.back_second()
        last.fill_inner(ACT_Q)
        ship_sums(G)
        for field in (FWD2, FWD1):
            take_halo(1, field)
        last.fill_margins(ACT_Q)
        last.advance_first()
        last.advance_second()
        keep_sums(G)
        ship_sums(F)
        keep_sums(F)

    @pl.when(even)
    def _():
        def put(field, value):
            if field < RET1:
                sent[1, field] = value
                pl.when(end_on)(end_move(field).start)
                pl.when(leaves)(leave_move(field).start)
            else:
                (ret_out, grd_out)[field // 2 - 1][field % 2] = value

        last = Tick(1, OTHER, put, lambda field: (ret_out, grd_out)[field // 2 - 1][field % 2])

        def arrive(field):
            if field < GRD1:
                mid_move(field).wait_recv()
            else:
                pl.when(above)(mid_move(field).wait_recv)
                if field == GRD2:
                    pl.when(leaves)(edge(2).wait)
            send_halo(1, field)

        @pl.when(straight)
        def _():
            arrive(RET2)
            arrive(RET1)
            last.fill_inner(ACT_Y)
            last.fill_inner(ACT_Q)
            for field in (FWD2, FWD1):
                take_halo(1, field)
            last.fill_margins(ACT_Q)
            pass_sums(OWN, G, late)
            pass_sums(OWN, F, early)
            take_halo(1, RET1)
            last.fill_margins(ACT_Y)
            take_weights(G)
            take_halo(1, RET2)
            last.invert_second()
            for part in range(pieces):
                spread_weights(F, part)
            arrive(GRD2)
            pass_sums(OWN, F, late)
            last.correlate_g()
            start_sums(OTHER, G)
            for part in range(pieces):
                pass_weights(F, part)
            take_weights(F)
            last.advance_first()
            last.fill_inner(GRAD2)
            take_halo(1, GRD2)
            last.fill_margins(GRAD2)
            pass_sums(OTHER, G)
            last.back_first()
            arrive(GRD1)
            last.back_inner()
            last.correlate_f()
            start_sums(OTHER, F)
            last.advance_second()

        @pl.when(shared)
        def _():
            arrive(GRD2)
            arrive(GRD1)
            last.fill_inner(GRAD2)
            last.fill_inner(ACT_Q)
            for part in range(pieces):
                pass_weights(F, part)
            for field in (FWD2, FWD1):
                take_halo(1, field)
            last.fill_margins(ACT_Q)
            take_weights(G)
            take_weights(F)
            last.advance_first()
            arrive(RET1)
            last.fill_inner(ACT_Y)
            last.advance_second()
            take_halo(1, RET1)
            last.fill_margins(ACT_Y)
            last.correlate_g()
            start_sums(OTHER, G)
            arrive(RET2)
            take_halo(1, GRD2)
            last.fill_margins(GRAD2)
            pass_sums(OWN, F, early)
            pass_sums(OTHER, G)
            last.back_first()
            last.back_inner()
            take_halo(1, RET2)
            last.invert_second()
            last.correlate_f()
            start_sums(OTHER, F)
            last.invert_first()

        pass_sums(OTHER, F)

        @pl.when(shared)
        def _():
            pass_sums(OWN, F, late)


        @pl.when(straight)
        def _():
            last.invert_first()

        take_halo(1, GRD1)
        last.back_margins()
        last.back_second()
        keep_sums(G)
        ship_sums(G)
        ship_sums(F)
        keep_sums(F)

    pl.when(first_seg)(edge(1).wait)
    pl.when(last_seg)(edge(3).wait)
    for field in (FWD1, FWD2):
        pl.when(jnp.logical_and(even, below))(end_move(field).wait_recv)
        pl.when(last_seg)(end_move(field + 2).wait_recv)
    for field in (RET1, RET2, GRD1, GRD2):
        pl.when(jnp.logical_and(odd, above))(end_move(field).wait_recv)

    for field in range(6):
        for tick in range(2):
            pl.when(jnp.logical_not(at_top))(halo_copy(tick, field, 0).wait_send)
            pl.when(jnp.logical_not(at_bottom))(halo_copy(tick, field, 1).wait_send)
        if field < RET1:
            pl.when(mid_on)(mid_move(field).wait_send)
            pl.when(last_seg)(turn_move(field).wait_send)
            pl.when(end_on)(end_move(field).wait_send)
            pl.when(leaves)(leave_move(field).wait_send)
        else:
            pl.when(mid_back)(mid_move(field).wait_send)
            pl.when(end_back)(end_move(field).wait_send)
    for index in range(2):
        for part in range(pieces):
            w_across(index, part).wait_send()
            for step in range(1, groups):
                w_group(index, part, step).wait_send()
            for step in range(groups):
                w_core(index, part, step).wait_send()
        for which in range(2):
            for target in range(groups):
                pair_copy(which, index, target).wait_send()
            for part in range(pieces):
                for step in range(1, groups):
                    reduce_copy(which, index, part, step).wait_send()

    close_sums(G)
    close_sums(F)
    for index in range(2):
        for part in range(pieces):
            ship_copy(index, part).wait_send()


def store(*refs):
    count = (len(refs) - 2) // 3
    sources, targets, held = refs[:count], refs[count:2 * count], refs[2 * count:3 * count]
    load_sem, store_sem = refs[3 * count:]
    parts = [(i, j) for i in reversed(range(count)) for j in range(held[i].shape[0])]
    loads = [pltpu.make_async_copy(sources[i].at[j], held[i].at[j], load_sem.at[i, j]) for i, j in parts]
    stores = [pltpu.make_async_copy(held[i].at[j], targets[i].at[j], store_sem.at[i, j]) for i, j in parts]
    for load in loads:
        load.start()
    for load, out in zip(loads, stores):
        load.wait()
        out.start()
    for out in stores:
        out.wait()


def local(forward_state, returning_state, returning_grad, weights, fresh_input, loss_grad):
    segments, bands = lax.axis_size("segment"), lax.axis_size("band")
    _, _, rows, width, channels = forward_state.shape
    pixels = rows * width
    taps = weights.shape[2]
    chunk = taps // bands
    groups = bands // 2
    pieces = next(count for count in (2, 1) if chunk % (16 * count) == 0 or count == 1)
    assert fresh_input.shape[0] == 2 and segments % 2 == 0 and bands % 2 == 0 and rows >= 2
    bf16, f32 = jnp.bfloat16, jnp.float32
    pair = jax.ShapeDtypeStruct((2, pixels, channels), bf16)
    dma = pltpu.SemaphoreType.DMA
    flat = lambda x: x.reshape(x.shape[:-3] + (pixels, channels))
    vmem = pl.BlockSpec(memory_space=pltpu.VMEM)
    outs = pl.pallas_call(
        functools.partial(kernel, segments, bands, width, pieces),
        out_shape=(pair, pair, pair, jax.ShapeDtypeStruct((2, chunk, channels), f32)),
        in_specs=[pl.BlockSpec(memory_space=pl.ANY)] * 6,
        out_specs=(vmem,) * 4,
        scratch_shapes=[
            pltpu.VMEM((2, 6, pixels + 4 * width, channels), bf16),
            pltpu.VMEM((2, 2, taps, channels), bf16),
            pltpu.VMEM((6, pixels + 4 * width, 3 * channels), bf16),
            pltpu.VMEM((2, 6, pixels, channels), bf16),
            pltpu.VMEM((pixels + 2 * width, channels), f32),
            pltpu.VMEM((2, 2, taps, channels), f32),
            pltpu.VMEM((2, 2, taps, channels), bf16),
            pltpu.VMEM((2, 2, groups, chunk, channels), bf16),
            pltpu.VMEM((2, 2, groups - 1, chunk, channels), bf16),
            pltpu.VMEM((2, 2, groups - 1, chunk, channels), bf16),
            pltpu.VMEM((2, chunk, channels), f32),
            pltpu.VMEM((2, chunk, channels), bf16),
            pltpu.VMEM((2, chunk, channels), bf16),
            dma((6,)),
            dma((2,)),
            dma((4,)),
            dma((2, 6, 2)),
            dma((2, 6, 2)),
            dma((6,)),
            dma((6,)),
            dma((6,)),
            dma((6,)),
            dma((2, pieces)),
            dma((2, pieces)),
            dma((2, pieces, groups - 1)),
            dma((2, pieces, groups - 1)),
            dma((2, pieces, groups)),
            dma((2, pieces, groups)),
            dma((2, 2, groups)),
            dma((2, 2, groups)),
            dma((2, 2, pieces, groups - 1)),
            dma((2, 2, pieces, groups - 1)),
            dma((2, pieces)),
            dma((2, pieces)),
        ],
        compiler_params=pltpu.CompilerParams(
            collective_id=0, has_side_effects=True, vmem_limit_bytes=60 * 2**20),
    )(flat(forward_state[0]), flat(returning_state[0]), flat(returning_grad[0]), weights[0],
      flat(fresh_input), flat(loss_grad))
    outs = pl.pallas_call(
        store,
        out_shape=tuple(jax.ShapeDtypeStruct(o.shape, o.dtype) for o in outs),
        in_specs=[pl.BlockSpec(memory_space=pl.ANY)] * 4,
        out_specs=(pl.BlockSpec(memory_space=pl.ANY),) * 4,
        scratch_shapes=[pltpu.VMEM(o.shape, o.dtype) for o in outs] + [dma((4, 2)), dma((4, 2))],
    )(*outs)
    shape = forward_state.shape
    return tuple(o.reshape(shape) for o in outs[:3]) + (outs[3][None],)


def solution(mesh):
    pair = P("segment", None, "band", None, None)
    whole = P(None, None, "band", None, None)
    return jax.shard_map(
        local,
        mesh=mesh,
        in_specs=(pair, pair, pair, P("segment", None, None, None), whole, whole),
        out_specs=(pair, pair, pair, P("segment", None, "band", None)),
        check_vma=False,
    )
```

```python
import functools

import jax
import jax.numpy as jnp
from jax import lax
from jax.experimental import pallas as pl
from jax.experimental.pallas import tpu as pltpu
from jax.sharding import PartitionSpec as P

MESH = pl.DeviceIdType.MESH
ACT_Q, ACT_OUT, ACT_Y, GRAD2, ACT_IN, BACK1 = range(6)
FWD1, FWD2, RET1, RET2, GRD1, GRD2 = range(6)
F, G = 0, 1
OWN, OTHER = 0, 1
TAKES = {ACT_Q: FWD2, ACT_Y: RET1, GRAD2: GRD2}
DEPTH = {FWD1: 1, FWD2: 2, RET1: 2, RET2: 1, GRD1: 1, GRD2: 2}


def kernel(segments, bands, width, pieces, fwd_in, ret_in, grd_in, weights_in, fresh_in, loss_in,
           fwd_out, ret_out, grd_out, wgrad_out,
           fields, wts, stack, sent, pulled, total, total_half, paired, reduced, partial, owned, ship_src, ship_dst,
           in_sem, w_sem, edge_sem, halo_send, halo_recv, mid_send, mid_recv, end_send, end_recv,
           wy_send, wy_recv, wx_send, wx_recv, wc_send, wc_recv,
           pair_send, pair_recv, red_send, red_recv, ship_send, ship_recv):
    seg = lax.axis_index("segment")
    band = lax.axis_index("band")
    pixels = sent.shape[2]
    channels = sent.shape[3]
    triple = 3 * channels
    chunk = partial.shape[3]
    margin = 2 * width
    inner = pl.ds(margin, pixels)
    first_pixels = pixels + 2 * width
    parity = lax.rem(seg, 2)
    even, odd = parity == 0, parity == 1
    other_seg = seg + 1 - 2 * parity
    first_seg, last_seg = seg == 0, seg == segments - 1
    below, above = seg >= 2, seg < segments - 2
    groups = bands // 2
    core, group = lax.rem(band, 2), band // 2
    core_band = band + 1 - 2 * core
    at_top, at_bottom = band == 0, band == bands - 1

    sources = {FWD1: fwd_in.at[0], FWD2: fwd_in.at[1], RET1: ret_in.at[0], RET2: ret_in.at[1],
               GRD1: grd_in.at[0], GRD2: grd_in.at[1]}

    def load(field):
        return pltpu.make_async_copy(sources[field], fields.at[0, field, inner], in_sem.at[field])

    def load_weights(index):
        return pltpu.make_async_copy(weights_in.at[index], wts.at[OWN, index], w_sem.at[index])

    load(RET1).start()
    load(GRD2).start()
    load_weights(G).start()
    load(RET2).start()
    load(GRD1).start()
    load_weights(F).start()
    load(FWD2).start()
    load(FWD1).start()

    barrier = pltpu.get_barrier_semaphore()
    for step in range(1, bands):
        pl.semaphore_signal(barrier, inc=1, device_id=(seg, lax.rem(band + step, bands)), device_id_type=MESH)
    pl.semaphore_signal(barrier, inc=1, device_id=(other_seg, band), device_id_type=MESH)

    @pl.when(below)
    def _():
        pl.semaphore_signal(barrier, inc=1, device_id=(seg - 2, band), device_id_type=MESH)

    @pl.when(above)
    def _():
        pl.semaphore_signal(barrier, inc=1, device_id=(seg + 2, band), device_id_type=MESH)

    def edge(which):
        return (
            pltpu.make_async_copy(fresh_in.at[0], fields.at[1, pl.ds(FWD1, 2), inner], edge_sem.at[0]),
            pltpu.make_async_copy(fresh_in.at[1], fwd_out, edge_sem.at[1]),
            pltpu.make_async_copy(loss_in.at[0], fields.at[1, pl.ds(GRD1, 2), inner], edge_sem.at[2]),
            pltpu.make_async_copy(loss_in.at[1], grd_out, edge_sem.at[3]),
        )[which]

    edge_places = (seg == 1, first_seg, seg == segments - 2, last_seg)
    for which in range(4):
        pl.when(edge_places[which])(edge(which).start)

    @pl.when(at_top)
    def _():
        fields[:, :, 0:margin] = jnp.zeros((2, 6, margin, channels), jnp.bfloat16)

    @pl.when(at_bottom)
    def _():
        fields[:, :, margin + pixels:] = jnp.zeros((2, 6, margin, channels), jnp.bfloat16)

    def halo_copy(tick, field, side):
        size = DEPTH[field] * width
        if side == 0:
            source, target = margin, margin + pixels
        else:
            source, target = margin + pixels - size, margin - size
        return pltpu.make_async_remote_copy(
            src_ref=fields.at[tick, field, pl.ds(source, size)], dst_ref=fields.at[tick, field, pl.ds(target, size)],
            send_sem=halo_send.at[tick, field, side], recv_sem=halo_recv.at[tick, field, 1 - side],
            device_id=(seg, band - 1 if side == 0 else band + 1), device_id_type=MESH)

    def send_halo(tick, field):
        pl.when(jnp.logical_not(at_top))(halo_copy(tick, field, 0).start)
        pl.when(jnp.logical_not(at_bottom))(halo_copy(tick, field, 1).start)

    def take_halo(tick, field):
        pl.when(jnp.logical_not(at_top))(halo_copy(tick, field, 1).wait_recv)
        pl.when(jnp.logical_not(at_bottom))(halo_copy(tick, field, 0).wait_recv)

    piece = chunk // pieces

    def w_rows(owner, part):
        return pl.ds(pl.multiple_of(owner * chunk + part * piece, piece), piece)

    def w_across(index, part):
        return pltpu.make_async_remote_copy(
            src_ref=wts.at[OWN, index, w_rows(band, part)], dst_ref=wts.at[OTHER, index, w_rows(band, part)],
            send_sem=wy_send.at[index, part], recv_sem=wy_recv.at[index, part],
            device_id=(other_seg, band), device_id_type=MESH)

    def w_group(index, part, step):
        rows = w_rows(band, part)
        return pltpu.make_async_remote_copy(
            src_ref=wts.at[OTHER, index, rows], dst_ref=wts.at[OTHER, index, rows],
            send_sem=wx_send.at[index, part, step - 1], recv_sem=wx_recv.at[index, part, step - 1],
            device_id=(seg, 2 * lax.rem(group + step, groups) + core), device_id_type=MESH)

    def w_core(index, part, step):
        rows = w_rows(2 * lax.rem(group + groups - step, groups) + core, part)
        return pltpu.make_async_remote_copy(
            src_ref=wts.at[OTHER, index, rows], dst_ref=wts.at[OTHER, index, rows],
            send_sem=wc_send.at[index, part, step], recv_sem=wc_recv.at[index, part, step],
            device_id=(seg, core_band), device_id_type=MESH)

    def w_direct(index, part, step):
        rows = w_rows(2 * lax.rem(group + groups - step, groups) + core, part)
        return pltpu.make_async_remote_copy(
            src_ref=wts.at[OWN, index, rows], dst_ref=wts.at[OTHER, index, rows],
            send_sem=wx_send.at[index, part, step - 1], recv_sem=wx_recv.at[index, part, step - 1],
            device_id=(other_seg, band), device_id_type=MESH)

    straight = jnp.logical_and(above, other_seg < segments - 2) if groups == 2 else jnp.bool_(False)

    def is_direct(index, part):
        if index == G or groups != 2:
            return jnp.bool_(False)
        return jnp.bool_(True) if part < pieces // 2 else straight

    def start_weights(index):
        for part in range(pieces):
            w_across(index, part).start()
        if index == F:
            for part in range(pieces):
                for step in range(1, groups):
                    pl.when(is_direct(index, part))(w_direct(index, part, step).start)

    def spread_weights(index, part):
        w_across(index, part).wait_recv()
        for step in range(1, groups):
            pl.when(jnp.logical_not(is_direct(index, part)))(w_group(index, part, step).start)
        w_core(index, part, 0).start()

    def pass_weights(index, part):
        for step in range(1, groups):
            w_group(index, part, step).wait_recv()
            w_core(index, part, step).start()

    def take_weights(index):
        for part in range(pieces):
            for step in range(groups):
                w_core(index, part, step).wait_recv()

    def fill(slot, value, start=0):
        rows = value.shape[0]
        column = lax.rem(lax.broadcasted_iota(jnp.int32, (rows, channels), 0), width)
        wide = value.astype(jnp.float32)
        left = jnp.where(column == 0, 0.0, pltpu.roll(wide, 1, 0))
        right = jnp.where(column == width - 1, 0.0, pltpu.roll(wide, rows - 1, 0))
        stack[slot, start:start + rows, 0:channels] = left.astype(jnp.bfloat16)
        stack[slot, start:start + rows, channels:2 * channels] = value
        stack[slot, start:start + rows, 2 * channels:triple] = right.astype(jnp.bfloat16)

    def conv(slot, weight, rows):
        result = None
        for row in range(3):
            term = jnp.dot(stack[slot, row * width:row * width + rows], weight[row * triple:(row + 1) * triple],
                           preferred_element_type=jnp.float32)
            result = term if result is None else result + term
        return result

    def back(slot, weight, rows):
        result = None
        for tap in range(9):
            row, col = tap // 3, tap % 3
            start = (8 - tap) * channels
            term = lax.dot_general(stack[slot, row * width:row * width + rows, col * channels:(col + 1) * channels],
                                   weight[start:start + channels], (((1,), (1,)), ((), ())),
                                   preferred_element_type=jnp.float32)
            result = term if result is None else result + term
        return result

    def correlate(which, index, slot, offset, grads):
        for row in range(3):
            start = offset + row * width
            term = lax.dot_general(stack[slot, start:start + pixels], grads, (((0,), (0,)), ((), ())),
                                   preferred_element_type=jnp.float32)
            rows = slice(row * triple, (row + 1) * triple)
            total[which, index, rows] = term
            total_half[which, index, rows] = term.astype(jnp.bfloat16)

    def act(value):
        wide = value.astype(jnp.float32)
        return (wide * jax.nn.sigmoid(wide)).astype(jnp.bfloat16)

    def slope(value):
        wide = value.astype(jnp.float32)
        sigmoid = jax.nn.sigmoid(wide)
        return sigmoid * (1.0 + wide * (1.0 - sigmoid))

    place = lax.broadcasted_iota(jnp.int32, (first_pixels, channels), 0)
    inside = jnp.logical_and(place >= jnp.where(at_top, width, 0),
                             place < jnp.where(at_bottom, width + pixels, first_pixels))

    def trim(value):
        return jnp.where(inside, value, 0.0).astype(jnp.bfloat16)

    grown = slice(width, margin + pixels + width)
    core_rows = slice(margin, margin + pixels)
    kept = slice(width, width + pixels)

    class Tick:
        def __init__(self, tick, which, put, got):
            self.tick, self.which, self.put, self.got = tick, which, put, got

        def field(self, name, rows=core_rows):
            return fields[self.tick, name, rows]

        def weight(self, index):
            return wts.at[self.which, index]

        def advance_first(self):
            out1 = trim(self.field(FWD1, grown).astype(jnp.float32) + conv(ACT_Q, self.weight(F), first_pixels))
            self.put(FWD1, out1[kept])
            fill(ACT_OUT, act(out1))

        def advance_second(self):
            out2 = self.field(FWD2).astype(jnp.float32) + conv(ACT_OUT, self.weight(G), pixels)
            self.put(FWD2, out2.astype(jnp.bfloat16))

        def fill_inner(self, slot):
            value = self.field(TAKES[slot])
            fill(slot, value if slot == GRAD2 else act(value), margin)

        def fill_margins(self, slot):
            for start in (0, margin + pixels):
                value = fields[self.tick, TAKES[slot], start:start + margin]
                fill(slot, value if slot == GRAD2 else act(value), start)

        def invert_second(self):
            q2 = trim(self.field(RET2, grown).astype(jnp.float32) - conv(ACT_Y, self.weight(G), first_pixels))
            self.put(RET2, q2[kept])
            fill(ACT_IN, act(q2))

        def back_first(self):
            pulled[...] = slope(self.field(RET1, grown)) * back(GRAD2, self.weight(G), first_pixels)

        def back_inner(self):
            h1 = (self.field(GRD1).astype(jnp.float32) + pulled[kept]).astype(jnp.bfloat16)
            self.put(GRD1, h1)
            fill(BACK1, h1, width)

        def back_margins(self):
            for start, outside in ((0, at_top), (width + pixels, at_bottom)):
                rows = slice(start, start + width)
                grad = fields[self.tick, GRD1, start + width:start + 2 * width].astype(jnp.float32)
                fill(BACK1, jnp.where(outside, 0.0, grad + pulled[rows]).astype(jnp.bfloat16), start)

        def invert_first(self):
            p2 = self.field(RET1).astype(jnp.float32) - conv(ACT_IN, self.weight(F), pixels)
            self.put(RET1, p2.astype(jnp.bfloat16))

        def back_second(self):
            h2 = (self.field(GRD2).astype(jnp.float32)
                  + slope(self.got(RET2)) * back(BACK1, self.weight(F), pixels))
            self.put(GRD2, h2.astype(jnp.bfloat16))

        def correlate_g(self):
            correlate(self.tick, G, ACT_Y, width, self.field(GRD2))

        def correlate_f(self):
            correlate(self.tick, F, ACT_IN, 0, self.got(GRD1))

    def move(tick, field, target, device):
        return pltpu.make_async_remote_copy(
            src_ref=sent.at[tick, field], dst_ref=target[0], send_sem=(mid_send, end_send)[tick].at[field],
            recv_sem=(mid_recv, end_recv)[tick].at[target[1]], device_id=(device, band), device_id_type=MESH)

    def mid_target(field):
        return fields.at[1, field, inner], field

    def end_target(field):
        return (fwd_out, ret_out, grd_out)[field // 2].at[field % 2], field

    def mid_move(field):
        return move(0, field, mid_target(field), seg + 2 if field < RET1 else seg - 2)

    def turn_move(field):
        return move(0, field, mid_target(field + 2), seg - 1)

    def end_move(field):
        return move(1, field, end_target(field), seg + 2 if field < RET1 else seg - 2)

    def leave_move(field):
        return move(1, field, end_target(field + 2), seg + 1)

    mid_back = jnp.logical_and(even, below)
    mid_on = jnp.logical_and(odd, above)
    end_on = jnp.logical_and(even, above)
    end_back = jnp.logical_and(odd, below)
    leaves = seg == segments - 2

    def send_mid(field):
        if field < RET1:
            pl.when(mid_on)(mid_move(field).start)
            pl.when(last_seg)(turn_move(field).start)
        else:
            pl.when(mid_back)(mid_move(field).start)

    def put_mid(field, value):
        sent[0, field] = value
        if field != GRD1:
            send_mid(field)

        @pl.when(even if field < RET1 else odd)
        def _():
            fields[1, field, core_rows] = value

    def chunk_rows(owner):
        return pl.ds(pl.multiple_of(owner * chunk, chunk), chunk)

    def pair_copy(which, index, target):
        return pltpu.make_async_remote_copy(
            src_ref=total_half.at[which, index, chunk_rows(2 * target + 1 - core)],
            dst_ref=paired.at[which, index, target],
            send_sem=pair_send.at[which, index, target], recv_sem=pair_recv.at[which, index, target],
            device_id=(seg, core_band), device_id_type=MESH)

    def reduce_copy(which, index, part, step):
        rows = pl.ds(part * piece, piece)
        return pltpu.make_async_remote_copy(
            src_ref=reduced.at[which, index, step - 1, rows], dst_ref=partial.at[which, index, step - 1, rows],
            send_sem=red_send.at[which, index, part, step - 1], recv_sem=red_recv.at[which, index, part, step - 1],
            device_id=(seg, 2 * lax.rem(group + step, groups) + core), device_id_type=MESH)

    def ship_copy(index, part):
        rows = pl.ds(part * piece, piece)
        return pltpu.make_async_remote_copy(
            src_ref=ship_src.at[index, rows], dst_ref=ship_dst.at[index, rows],
            send_sem=ship_send.at[index, part], recv_sem=ship_recv.at[index, part],
            device_id=(other_seg, band), device_id_type=MESH)

    def start_sums(which, index):
        for target in range(groups):
            pair_copy(which, index, target).start()

    def pair_sum(which, index, target, part):
        rows = pl.ds(part * piece, piece)
        return (total[which, index, w_rows(2 * target + core, part)]
                + paired[which, index, target, rows].astype(jnp.float32))

    early, late = range((pieces + 1) // 2), range((pieces + 1) // 2, pieces)

    def pass_sums(which, index, parts=range(pieces)):
        if 0 in parts:
            for target in range(groups):
                pair_copy(which, index, target).wait_recv()
        for part in parts:
            rows = pl.ds(part * piece, piece)
            for step in range(1, groups):
                value = pair_sum(which, index, lax.rem(group + step, groups), part)
                reduced[which, index, step - 1, rows] = value.astype(jnp.bfloat16)
                reduce_copy(which, index, part, step).start()

    def finish_sums(which, index, part):
        value = pair_sum(which, index, group, part)
        for step in range(1, groups):
            reduce_copy(which, index, part, step).wait_recv()
            value = value + partial[which, index, step - 1, pl.ds(part * piece, piece)].astype(jnp.float32)
        return value

    def keep_sums(index):
        for part in range(pieces):
            owned[index, pl.ds(part * piece, piece)] = finish_sums(OWN, index, part)

    def ship_sums(index):
        for part in range(pieces):
            ship_src[index, pl.ds(part * piece, piece)] = finish_sums(OTHER, index, part).astype(jnp.bfloat16)
            ship_copy(index, part).start()

    def close_sums(index):
        for part in range(pieces):
            rows = pl.ds(part * piece, piece)
            ship_copy(index, part).wait_recv()
            wgrad_out[index, rows] = owned[index, rows] + ship_dst[index, rows].astype(jnp.float32)

    first = Tick(0, OWN, put_mid, lambda field: sent[0, field])
    load(RET1).wait()
    first.fill_inner(ACT_Y)
    load(GRD2).wait()
    first.fill_inner(GRAD2)
    load(FWD2).wait()
    first.fill_inner(ACT_Q)
    load(RET2).wait()
    load(GRD1).wait()
    load(FWD1).wait()
    load_weights(G).wait()
    load_weights(F).wait()
    neighbours = below.astype(jnp.int32) + above.astype(jnp.int32)
    pl.semaphore_wait(barrier, bands + neighbours)
    for field in (RET1, RET2, GRD2, GRD1, FWD2, FWD1):
        send_halo(0, field)
    start_weights(G)
    start_weights(F)

    take_halo(0, RET1)
    first.fill_margins(ACT_Y)
    take_halo(0, RET2)
    first.invert_second()
    take_halo(0, GRD2)
    first.fill_margins(GRAD2)
    first.back_first()
    take_halo(0, GRD1)
    first.back_inner()
    first.back_margins()
    spread_weights(G, 0)
    first.invert_first()
    first.back_second()
    send_mid(GRD1)

    @pl.when(odd)
    def _():
        for field in (RET1, RET2, GRD2, GRD1):
            send_halo(1, field)

    first.correlate_g()
    start_sums(OWN, G)
    for part in range(1, pieces):
        spread_weights(G, part)
    first.correlate_f()
    start_sums(OWN, F)
    shared = jnp.logical_not(straight)

    @pl.when(jnp.logical_and(straight, even))
    def _():
        pass_sums(OWN, G, early)

    @pl.when(shared)
    def _():
        spread_weights(F, 0)

    take_halo(0, FWD2)
    first.fill_margins(ACT_Q)
    take_halo(0, FWD1)
    first.advance_first()

    @pl.when(shared)
    def _():
        for part in range(1, pieces):
            spread_weights(F, part)

    @pl.when(jnp.logical_and(straight, odd))
    def _():
        pass_sums(OWN, G)
        pass_sums(OWN, F)

    for part in range(pieces):
        pass_weights(G, part)
    first.advance_second()

    @pl.when(even)
    def _():
        for field in (FWD2, FWD1):
            send_halo(1, field)

    @pl.when(shared)
    def _():
        pass_sums(OWN, G)

    @pl.when(odd)
    def _():
        def put(field, value):
            if field < RET1:
                fwd_out[field] = value
            else:
                sent[1, field] = value
                pl.when(end_back)(end_move(field).start)

        last = Tick(1, OTHER, put, lambda field: sent[1, field])
        last.fill_inner(ACT_Y)
        last.fill_inner(GRAD2)
        take_halo(1, RET1)
        last.fill_margins(ACT_Y)
        take_halo(1, GRD2)
        last.fill_margins(GRAD2)
        last.correlate_g()
        start_sums(OTHER, G)
        take_halo(1, RET2)
        take_halo(1, GRD1)
        take_weights(G)
        last.invert_second()
        last.back_first()
        last.back_inner()
        last.back_margins()
        pass_sums(OTHER, G)
        last.correlate_f()
        start_sums(OTHER, F)

        @pl.when(straight)
        def _():
            for part in range(pieces):
                spread_weights(F, part)

        for field in (FWD2, FWD1):
            pl.when(below)(mid_move(field).wait_recv)
        pl.when(seg == 1)(edge(0).wait)
        for field in (FWD2, FWD1):
            send_halo(1, field)
        for part in range(pieces):
            pass_weights(F, part)
        pass_sums(OTHER, F)

        @pl.when(shared)
        def _():
            pass_sums(OWN, F)


        take_weights(F)
        last.invert_first()
        last.back_second()
        last.fill_inner(ACT_Q)
        ship_sums(G)
        for field in (FWD2, FWD1):
            take_halo(1, field)
        last.fill_margins(ACT_Q)
        last.advance_first()
        last.advance_second()
        keep_sums(G)
        ship_sums(F)
        keep_sums(F)

    @pl.when(even)
    def _():
        def put(field, value):
            if field < RET1:
                sent[1, field] = value
                pl.when(end_on)(end_move(field).start)
                pl.when(leaves)(leave_move(field).start)
            else:
                (ret_out, grd_out)[field // 2 - 1][field % 2] = value

        last = Tick(1, OTHER, put, lambda field: (ret_out, grd_out)[field // 2 - 1][field % 2])

        def arrive(field):
            if field < GRD1:
                mid_move(field).wait_recv()
            else:
                pl.when(above)(mid_move(field).wait_recv)
                if field == GRD2:
                    pl.when(leaves)(edge(2).wait)
            send_halo(1, field)

        @pl.when(straight)
        def _():
            arrive(RET2)
            arrive(RET1)
            last.fill_inner(ACT_Y)
            last.fill_inner(ACT_Q)
            for field in (FWD2, FWD1):
                take_halo(1, field)
            last.fill_margins(ACT_Q)
            pass_sums(OWN, G, late)
            pass_sums(OWN, F, early)
            take_halo(1, RET1)
            last.fill_margins(ACT_Y)
            take_weights(G)
            take_halo(1, RET2)
            last.invert_second()
            for part in range(pieces):
                spread_weights(F, part)
            arrive(GRD2)
            pass_sums(OWN, F, late)
            last.correlate_g()
            start_sums(OTHER, G)
            for part in range(pieces):
                pass_weights(F, part)
            take_weights(F)
            last.advance_first()
            last.fill_inner(GRAD2)
            take_halo(1, GRD2)
            last.fill_margins(GRAD2)
            pass_sums(OTHER, G)
            last.back_first()
            arrive(GRD1)
            last.back_inner()
            last.correlate_f()
            start_sums(OTHER, F)
            last.advance_second()

        @pl.when(shared)
        def _():
            arrive(GRD2)
            arrive(GRD1)
            last.fill_inner(GRAD2)
            last.fill_inner(ACT_Q)
            for part in range(pieces):
                pass_weights(F, part)
            for field in (FWD2, FWD1):
                take_halo(1, field)
            last.fill_margins(ACT_Q)
            take_weights(G)
            take_weights(F)
            last.advance_first()
            arrive(RET1)
            last.fill_inner(ACT_Y)
            last.advance_second()
            take_halo(1, RET1)
            last.fill_margins(ACT_Y)
            last.correlate_g()
            start_sums(OTHER, G)
            arrive(RET2)
            take_halo(1, GRD2)
            last.fill_margins(GRAD2)
            pass_sums(OWN, F, early)
            pass_sums(OTHER, G)
            last.back_first()
            last.back_inner()
            take_halo(1, RET2)
            last.invert_second()
            last.correlate_f()
            start_sums(OTHER, F)
            last.invert_first()

        pass_sums(OTHER, F)

        @pl.when(shared)
        def _():
            pass_sums(OWN, F, late)


        @pl.when(straight)
        def _():
            last.invert_first()

        take_halo(1, GRD1)
        last.back_margins()
        last.back_second()
        keep_sums(G)
        ship_sums(G)
        ship_sums(F)
        keep_sums(F)

    pl.when(first_seg)(edge(1).wait)
    pl.when(last_seg)(edge(3).wait)
    for field in (FWD1, FWD2):
        pl.when(jnp.logical_and(even, below))(end_move(field).wait_recv)
        pl.when(last_seg)(end_move(field + 2).wait_recv)
    for field in (RET1, RET2, GRD1, GRD2):
        pl.when(jnp.logical_and(odd, above))(end_move(field).wait_recv)

    for field in range(6):
        for tick in range(2):
            pl.when(jnp.logical_not(at_top))(halo_copy(tick, field, 0).wait_send)
            pl.when(jnp.logical_not(at_bottom))(halo_copy(tick, field, 1).wait_send)
        if field < RET1:
            pl.when(mid_on)(mid_move(field).wait_send)
            pl.when(last_seg)(turn_move(field).wait_send)
            pl.when(end_on)(end_move(field).wait_send)
            pl.when(leaves)(leave_move(field).wait_send)
        else:
            pl.when(mid_back)(mid_move(field).wait_send)
            pl.when(end_back)(end_move(field).wait_send)
    for index in range(2):
        for part in range(pieces):
            w_across(index, part).wait_send()
            for step in range(1, groups):
                w_group(index, part, step).wait_send()
            for step in range(groups):
                w_core(index, part, step).wait_send()
        for which in range(2):
            for target in range(groups):
                pair_copy(which, index, target).wait_send()
            for part in range(pieces):
                for step in range(1, groups):
                    reduce_copy(which, index, part, step).wait_send()

    close_sums(G)
    close_sums(F)
    for index in range(2):
        for part in range(pieces):
            ship_copy(index, part).wait_send()


def store(*refs):
    count = (len(refs) - 2) // 3
    sources, targets, held = refs[:count], refs[count:2 * count], refs[2 * count:3 * count]
    load_sem, store_sem = refs[3 * count:]
    parts = [(i, j) for i in reversed(range(count)) for j in range(held[i].shape[0])]
    loads = [pltpu.make_async_copy(sources[i].at[j], held[i].at[j], load_sem.at[i, j]) for i, j in parts]
    stores = [pltpu.make_async_copy(held[i].at[j], targets[i].at[j], store_sem.at[i, j]) for i, j in parts]
    for load in loads:
        load.start()
    for load, out in zip(loads, stores):
        load.wait()
        out.start()
    for out in stores:
        out.wait()


def local(forward_state, returning_state, returning_grad, weights, fresh_input, loss_grad):
    segments, bands = lax.axis_size("segment"), lax.axis_size("band")
    _, _, rows, width, channels = forward_state.shape
    pixels = rows * width
    taps = weights.shape[2]
    chunk = taps // bands
    groups = bands // 2
    pieces = next(count for count in (2, 1) if chunk % (16 * count) == 0 or count == 1)
    assert fresh_input.shape[0] == 2 and segments % 2 == 0 and bands % 2 == 0 and rows >= 2
    bf16, f32 = jnp.bfloat16, jnp.float32
    pair = jax.ShapeDtypeStruct((2, pixels, channels), bf16)
    dma = pltpu.SemaphoreType.DMA
    flat = lambda x: x.reshape(x.shape[:-3] + (pixels, channels))
    vmem = pl.BlockSpec(memory_space=pltpu.VMEM)
    outs = pl.pallas_call(
        functools.partial(kernel, segments, bands, width, pieces),
        out_shape=(pair, pair, pair, jax.ShapeDtypeStruct((2, chunk, channels), f32)),
        in_specs=[pl.BlockSpec(memory_space=pl.ANY)] * 6,
        out_specs=(vmem,) * 4,
        scratch_shapes=[
            pltpu.VMEM((2, 6, pixels + 4 * width, channels), bf16),
            pltpu.VMEM((2, 2, taps, channels), bf16),
            pltpu.VMEM((6, pixels + 4 * width, 3 * channels), bf16),
            pltpu.VMEM((2, 6, pixels, channels), bf16),
            pltpu.VMEM((pixels + 2 * width, channels), f32),
            pltpu.VMEM((2, 2, taps, channels), f32),
            pltpu.VMEM((2, 2, taps, channels), bf16),
            pltpu.VMEM((2, 2, groups, chunk, channels), bf16),
            pltpu.VMEM((2, 2, groups - 1, chunk, channels), bf16),
            pltpu.VMEM((2, 2, groups - 1, chunk, channels), bf16),
            pltpu.VMEM((2, chunk, channels), f32),
            pltpu.VMEM((2, chunk, channels), bf16),
            pltpu.VMEM((2, chunk, channels), bf16),
            dma((6,)),
            dma((2,)),
            dma((4,)),
            dma((2, 6, 2)),
            dma((2, 6, 2)),
            dma((6,)),
            dma((6,)),
            dma((6,)),
            dma((6,)),
            dma((2, pieces)),
            dma((2, pieces)),
            dma((2, pieces, groups - 1)),
            dma((2, pieces, groups - 1)),
            dma((2, pieces, groups)),
            dma((2, pieces, groups)),
            dma((2, 2, groups)),
            dma((2, 2, groups)),
            dma((2, 2, pieces, groups - 1)),
            dma((2, 2, pieces, groups - 1)),
            dma((2, pieces)),
            dma((2, pieces)),
        ],
        compiler_params=pltpu.CompilerParams(
            collective_id=0, has_side_effects=True, vmem_limit_bytes=60 * 2**20),
    )(flat(forward_state[0]), flat(returning_state[0]), flat(returning_grad[0]), weights[0],
      flat(fresh_input), flat(loss_grad))
    outs = pl.pallas_call(
        store,
        out_shape=tuple(jax.ShapeDtypeStruct(o.shape, o.dtype) for o in outs),
        in_specs=[pl.BlockSpec(memory_space=pl.ANY)] * 4,
        out_specs=(pl.BlockSpec(memory_space=pl.ANY),) * 4,
        scratch_shapes=[pltpu.VMEM(o.shape, o.dtype) for o in outs] + [dma((4, 2)), dma((4, 2))],
    )(*outs)
    shape = forward_state.shape
    return tuple(o.reshape(shape) for o in outs[:3]) + (outs[3][None],)


def solution(mesh):
    pair = P("segment", None, "band", None, None)
    whole = P(None, None, "band", None, None)
    return jax.shard_map(
        local,
        mesh=mesh,
        in_specs=(pair, pair, pair, P("segment", None, None, None), whole, whole),
        out_specs=(pair, pair, pair, P("segment", None, "band", None)),
        check_vma=False,
    )
```
